32 devices in a mesh: row: 8 (over z, y), col: 4 (over x, core).
Axes of the slice: x: 2, y: 2, z: 4, core: 2. Of those that a mesh axis runs over, the one named last changes fastest.
Arguments:
- signal: bfloat16 [8, 256, 512], P(None, 'row', 'col'), may hold values from -6 to 6
- filter_real: bfloat16 [8, 256, 512], P(None, 'row', 'col'), may hold values from -6 to 6
- filter_imag: bfloat16 [8, 256, 512], P(None, 'row', 'col'), may hold values from -6 to 6
- skip: float32 [8], replicated, may hold values from 0.5 to 1.5
Outputs:
- output: bfloat16 [8, 256, 512], P(None, 'row', 'col')
The draws below stay inside these ranges and needn't reach their ends.
All inputs are finite; a program needn't handle non-finite values.
Results may differ from the reference program's by a relative error of at most 0.0064.
Values may be sent and summed in bfloat16 or wider, within the bound.
No kernel may reach another device: no remote copies, remote signals or barrier semaphores. Data moves between devices by JAX's collectives and lax.ppermute only.
A program may use at most 64 MiB of HBM per device.

```python
import math
import jax
import jax.numpy as jnp
from jax import lax

CHANNELS = 8
N1 = 256
N2 = 512


def levels(rng, shape, cuts, smallest, largest):
    level, own = 1.0, jax.random.fold_in(rng, 6)
    for axis_at, blocks in cuts:
        draws = jnp.exp(jax.random.uniform(jax.random.fold_in(own, axis_at), (blocks,), jnp.float32, smallest / len(cuts), largest / len(cuts)))
        level = level * jnp.repeat(draws, shape[axis_at] // blocks).reshape([-1 if axis == axis_at else 1 for axis in range(len(shape))])
    return level


def normal_values(own_key, dims, scale, most, cuts=(), kind=jnp.bfloat16):
    entries = jax.random.normal(own_key, dims, jnp.float32) * scale
    if len(cuts) > 0:
        entries = levels(own_key, dims, cuts, -0.22, 0.18) * entries
    return jnp.clip(entries, min=-most, max=most).astype(kind)


def setup_inputs(seed: int = 0) -> dict:
    key_list = jax.random.split(jax.random.key(seed), 5)
    signal = normal_values(key_list[0], (CHANNELS, N1, N2), 1.0, 6.0, ((1, 8), (2, 4)))
    filter_real = normal_values(key_list[1], (CHANNELS, N1, N2), 1.0, 6.0, ((1, 8), (2, 4)))
    filter_imag = normal_values(key_list[2], (CHANNELS, N1, N2), 1.0, 6.0, ((1, 8), (2, 4)))
    skip = jnp.clip(jax.random.uniform(key_list[3], (CHANNELS,), jnp.float32, 0.5, 1.5), 0.5, 1.5)
    return dict(signal=signal, filter_real=filter_real, filter_imag=filter_imag, skip=skip)


def phase_table(left_ids, right_ids, modulus):
    product = (left_ids[:, None] * right_ids[None, :]) % modulus
    angle = (-2.0 * math.pi / modulus) * product.astype(jnp.float32)
    return jnp.cos(angle), jnp.sin(angle)


def rounded(matrix):
    return lax.optimization_barrier(matrix.astype(jnp.bfloat16)).astype(jnp.float32)


def matmul(left, right):
    return jnp.dot(left, right, preferred_element_type=jnp.float32, precision=lax.Precision.HIGHEST)


def reference(signal, filter_real, filter_imag, skip):
    first_len = signal.shape[1]
    second_len = signal.shape[2]
    seq_len = first_len * second_len
    row_ids = jnp.arange(first_len, dtype=jnp.int32)
    col_ids = jnp.arange(second_len, dtype=jnp.int32)
    first_re, first_im = phase_table(row_ids, row_ids, first_len)
    first_re = rounded(first_re)
    first_im = rounded(first_im)
    second_re, second_im = phase_table(col_ids, col_ids, second_len)
    second_re = rounded(second_re)
    second_im = rounded(second_im)
    twist_re, twist_im = phase_table(row_ids, col_ids, seq_len)

    def one_channel(members):
        series = members[0].astype(jnp.float32)
        filt_re = members[1].astype(jnp.float32)
        filt_im = members[2].astype(jnp.float32)
        col_re = matmul(first_re, series)
        col_im = matmul(first_im, series)
        mixed_re = rounded(col_re * twist_re - col_im * twist_im)
        mixed_im = rounded(col_re * twist_im + col_im * twist_re)
        spec_re = matmul(mixed_re, second_re) - matmul(mixed_im, second_im)
        spec_im = matmul(mixed_re, second_im) + matmul(mixed_im, second_re)
        prod_re = rounded(spec_re * filt_re - spec_im * filt_im)
        prod_im = rounded(spec_re * filt_im + spec_im * filt_re)
        back_re = matmul(prod_re, second_re) + matmul(prod_im, second_im)
        back_im = matmul(prod_im, second_re) - matmul(prod_re, second_im)
        unwound_re = rounded(back_re * twist_re + back_im * twist_im)
        unwound_im = rounded(back_im * twist_re - back_re * twist_im)
        total = matmul(first_re, unwound_re) + matmul(first_im, unwound_im)
        return (total / seq_len + members[3] * series).astype(jnp.bfloat16)

    return lax.map(one_channel, (signal, filter_real, filter_imag, skip))
```

```python
import functools
import math

import jax
import jax.numpy as jnp
import numpy as np
from jax import lax
from jax.experimental import pallas as pl
from jax.experimental.pallas import tpu as pltpu
from jax.sharding import PartitionSpec as P


def phase_table(left_ids, right_ids, modulus):
    product = left_ids[:, None] * right_ids[None, :] % modulus
    angle = -2.0 * math.pi / modulus * product.astype(jnp.float32)
    return (jnp.cos(angle).astype(jnp.bfloat16), jnp.sin(angle).astype(jnp.bfloat16))


def twist_table(left_ids, right_ids, modulus):
    product = left_ids[:, None] * right_ids[None, :] % modulus
    angle = -2.0 * math.pi / modulus * product.astype(jnp.float32)
    return (jnp.cos(angle), jnp.sin(angle))


def column_product(series, phase):
    return jnp.einsum("crn,nk->crk", series, phase, preferred_element_type=jnp.float32)


def row_product(phase, series):
    return jnp.einsum("rn,cnj->crj", phase, series, preferred_element_type=jnp.float32)


def local_by_columns(signal, filter_real, filter_imag, skip):
    channels, row_count, col_count = signal.shape
    first_len = row_count * lax.axis_size("row")
    second_len = col_count * lax.axis_size("col")
    seq_len = first_len * second_len
    row_offset = lax.axis_index("row") * row_count
    col_offset = lax.axis_index("col") * col_count
    own_rows = row_offset + jnp.arange(row_count, dtype=jnp.int32)
    own_cols = col_offset + jnp.arange(col_count, dtype=jnp.int32)
    twist_re, twist_im = twist_table(own_rows, own_cols, seq_len)
    pair_width = col_count // lax.axis_size("row")
    pair_cols = (
        col_offset + lax.axis_index("row") * pair_width + jnp.arange(pair_width, dtype=jnp.int32)
    )
    all_rows = jnp.arange(first_len, dtype=jnp.int32)
    full_re, full_im = phase_table(all_rows, all_rows, first_len)
    columns_whole = lax.all_to_all(signal, "row", split_axis=2, concat_axis=1, tiled=True)
    pair_b_re = row_product(full_re, columns_whole)
    pair_b_im = row_product(full_im, columns_whole)
    pair_tw_re, pair_tw_im = twist_table(all_rows, pair_cols, seq_len)
    pair_mix_re = (pair_b_re * pair_tw_re - pair_b_im * pair_tw_im).astype(jnp.bfloat16)
    pair_mix_im = (pair_b_re * pair_tw_im + pair_b_im * pair_tw_re).astype(jnp.bfloat16)
    mixed_re, mixed_im = (
        lax.all_to_all(pair_mix_re, "row", split_axis=1, concat_axis=2, tiled=True),
        lax.all_to_all(pair_mix_im, "row", split_axis=1, concat_axis=2, tiled=True),
    )
    part_re = lax.all_gather(mixed_re, "col", axis=2, tiled=True)
    part_im = lax.all_gather(mixed_im, "col", axis=2, tiled=True)
    all_cols = jnp.arange(second_len, dtype=jnp.int32)
    phase_re, phase_im = phase_table(all_cols, own_cols, second_len)
    spec_re = column_product(part_re, phase_re) - column_product(part_im, phase_im)
    spec_im = column_product(part_re, phase_im) + column_product(part_im, phase_re)
    prod_re = (spec_re * filter_real - spec_im * filter_imag).astype(jnp.bfloat16)
    prod_im = (spec_re * filter_imag + spec_im * filter_real).astype(jnp.bfloat16)
    part_re = lax.all_gather(prod_re, "col", axis=2, tiled=True)
    part_im = lax.all_gather(prod_im, "col", axis=2, tiled=True)
    new_re = column_product(part_re, phase_re) + column_product(part_im, phase_im)
    new_im = column_product(part_im, phase_re) - column_product(part_re, phase_im)
    unwound_re = (new_re * twist_re + new_im * twist_im).astype(jnp.bfloat16)
    unwound_im = (new_im * twist_re - new_re * twist_im).astype(jnp.bfloat16)
    pair_un_re, pair_un_im = (
        lax.all_to_all(unwound_re, "row", split_axis=2, concat_axis=1, tiled=True),
        lax.all_to_all(unwound_im, "row", split_axis=2, concat_axis=1, tiled=True),
    )
    pair_total = row_product(full_re, pair_un_re) + row_product(full_im, pair_un_im)
    pair_out = (
        pair_total / seq_len + skip[:, None, None] * columns_whole.astype(jnp.float32)
    ).astype(jnp.bfloat16)
    return lax.all_to_all(pair_out, "row", split_axis=1, concat_axis=2, tiled=True)


def numpy_phase(left_ids, right_ids, modulus):
    product = (left_ids[:, None].astype(np.int64) * right_ids[None, :]) % modulus
    angle = np.float32(-2.0 * math.pi / modulus) * product.astype(np.float32)
    return np.cos(angle), np.sin(angle)


def tables(first_len, second_len, row_count, parts):
    height = row_count // parts
    rows = np.arange(first_len)
    cols = np.arange(second_len)
    first = np.stack(numpy_phase(rows, rows, first_len))
    twist = np.stack(numpy_phase(rows, cols, first_len * second_len))

    def by_part(table):
        width = table.shape[-1]
        cut = table.reshape(2, first_len // row_count, parts, height, width)
        return cut.transpose(2, 0, 1, 3, 4).reshape(parts, -1, width)

    second = np.concatenate(numpy_phase(cols, cols, second_len), axis=1)
    return (
        jnp.asarray(by_part(first), jnp.bfloat16),
        jnp.asarray(by_part(twist), jnp.float32),
        jnp.asarray(second, jnp.bfloat16),
    )


def spectrum_kernel(part_ref, got_ref, first_ref, twist_ref, second_ref, out_ref, *, rows, parts, row_count):
    del part_ref
    height = row_count // parts
    mine = rows * height
    first_len = rows * row_count
    col_count = got_ref.shape[-1]
    second_len = parts * col_count
    seq_len = first_len * second_len
    first = first_ref[0]
    twist_re = twist_ref[0, :mine]
    twist_im = twist_ref[0, mine:]

    def dot(left, right, dims=((1,), (0,))):
        return lax.dot_general(left, right, (dims, ((), ())), preferred_element_type=jnp.float32)

    series = jnp.concatenate(
        [got_ref[:, part, :row_count, :].reshape(first_len, col_count) for part in range(parts)], axis=1
    )
    half = dot(first, series)
    half_re, half_im = half[:mine], half[mine:]
    mixed = jnp.concatenate(
        [half_re * twist_re - half_im * twist_im, half_re * twist_im + half_im * twist_re], axis=0
    ).astype(jnp.bfloat16)
    both = dot(mixed, second_ref[...])
    spec_re = both[:mine, :second_len] - both[mine:, second_len:]
    spec_im = both[:mine, second_len:] + both[mine:, :second_len]

    def filter_part(start):
        return jnp.concatenate(
            [
                got_ref[:, part, start : start + height, :].astype(jnp.float32).reshape(mine, col_count)
                for part in range(parts)
            ],
            axis=1,
        )

    filt_re = filter_part(row_count)
    filt_im = filter_part(row_count + height)
    prod = jnp.concatenate(
        [spec_re * filt_re - spec_im * filt_im, spec_re * filt_im + spec_im * filt_re], axis=0
    ).astype(jnp.bfloat16)
    both = dot(prod, second_ref[...])
    back_re = both[:mine, :second_len] + both[mine:, second_len:]
    back_im = both[mine:, :second_len] - both[:mine, second_len:]
    unwound = jnp.concatenate(
        [back_re * twist_re + back_im * twist_im, back_im * twist_re - back_re * twist_im], axis=0
    ).astype(jnp.bfloat16)
    total = dot(first, unwound, ((0,), (0,))) / seq_len
    total = total.astype(jnp.bfloat16)
    for part in range(parts):
        piece = total[:, part * col_count : (part + 1) * col_count]
        out_ref[:, part] = piece.reshape(rows, row_count, col_count)


def local_by_channels(signal, filter_real, filter_imag, skip):
    channels, row_count, col_count = signal.shape
    rows = lax.axis_size("row")
    parts = lax.axis_size("col")
    share = channels // rows
    height = row_count // parts
    first, twist, second = tables(rows * row_count, parts * col_count, row_count, parts)
    part = lax.axis_index("col").astype(jnp.int32).reshape(1)
    outs = []
    for turn in range(share):
        own = slice(turn * rows, (turn + 1) * rows)
        send = jnp.concatenate(
            [
                jnp.broadcast_to(signal[own][:, None], (rows, parts, row_count, col_count)),
                filter_real[own].reshape(rows, parts, height, col_count),
                filter_imag[own].reshape(rows, parts, height, col_count),
            ],
            axis=2,
        )
        tall = send.shape[2]
        got = lax.all_to_all(
            send.reshape(rows * parts, tall, col_count), ("row", "col"), 0, 0, tiled=True
        ).reshape(rows, parts, tall, col_count)
        kernel = functools.partial(spectrum_kernel, rows=rows, parts=parts, row_count=row_count)
        partial_sums = pl.pallas_call(
            kernel,
            out_shape=jax.ShapeDtypeStruct((rows, parts, row_count, col_count), jnp.bfloat16),
            grid_spec=pltpu.PrefetchScalarGridSpec(
                num_scalar_prefetch=1,
                grid=(1,),
                in_specs=[
                    pl.BlockSpec(got.shape, lambda i, p: (0, 0, 0, 0)),
                    pl.BlockSpec((1,) + first.shape[1:], lambda i, p: (p[0], 0, 0)),
                    pl.BlockSpec((1,) + twist.shape[1:], lambda i, p: (p[0], 0, 0)),
                    pl.BlockSpec(second.shape, lambda i, p: (0, 0)),
                ],
                out_specs=pl.BlockSpec((rows, parts, row_count, col_count), lambda i, p: (0, 0, 0, 0)),
            ),
        )(part, got, first, twist, second)
        back = lax.all_to_all(
            partial_sums.reshape(rows * parts, row_count, col_count), ("row", "col"), 0, 0, tiled=True
        ).reshape(rows, parts, row_count, col_count)
        total = jnp.sum(back.astype(jnp.float32), axis=1)
        outs.append((total + skip[own, None, None] * signal[own].astype(jnp.float32)).astype(jnp.bfloat16))
    return outs[0] if share == 1 else jnp.concatenate(outs, axis=0)


def local(signal, filter_real, filter_imag, skip):
    channels, row_count, _ = signal.shape
    whole_shares = channels % lax.axis_size("row") == 0
    if whole_shares and row_count % (8 * lax.axis_size("col")) == 0:
        return local_by_channels(signal, filter_real, filter_imag, skip)
    return local_by_columns(signal, filter_real, filter_imag, skip)


def solution(mesh):
    in_specs = (P(None, "row", "col"), P(None, "row", "col"), P(None, "row", "col"), P())
    out_specs = P(None, "row", "col")
    return jax.shard_map(local, mesh=mesh, in_specs=in_specs, out_specs=out_specs, check_vma=False)
```

```python
import math

import jax
import jax.numpy as jnp
import numpy as np
from jax import lax
from jax.experimental import pallas as pl
from jax.experimental.pallas import tpu as pltpu
from jax.sharding import PartitionSpec as P


def phase_table(left_ids, right_ids, modulus):
    product = left_ids[:, None] * right_ids[None, :] % modulus
    angle = -2.0 * math.pi / modulus * product.astype(jnp.float32)
    return (jnp.cos(angle).astype(jnp.bfloat16), jnp.sin(angle).astype(jnp.bfloat16))


def twist_table(left_ids, right_ids, modulus):
    product = left_ids[:, None] * right_ids[None, :] % modulus
    angle = -2.0 * math.pi / modulus * product.astype(jnp.float32)
    return (jnp.cos(angle), jnp.sin(angle))


def column_product(series, phase):
    return jnp.einsum("crn,nk->crk", series, phase, preferred_element_type=jnp.float32)


def row_product(phase, series):
    return jnp.einsum("rn,cnj->crj", phase, series, preferred_element_type=jnp.float32)


def local_by_columns(signal, filter_real, filter_imag, skip):
    channels, row_count, col_count = signal.shape
    first_len = row_count * lax.axis_size("row")
    second_len = col_count * lax.axis_size("col")
    seq_len = first_len * second_len
    row_offset = lax.axis_index("row") * row_count
    col_offset = lax.axis_index("col") * col_count
    own_rows = row_offset + jnp.arange(row_count, dtype=jnp.int32)
    own_cols = col_offset + jnp.arange(col_count, dtype=jnp.int32)
    twist_re, twist_im = twist_table(own_rows, own_cols, seq_len)
    pair_width = col_count // lax.axis_size("row")
    pair_cols = (
        col_offset + lax.axis_index("row") * pair_width + jnp.arange(pair_width, dtype=jnp.int32)
    )
    all_rows = jnp.arange(first_len, dtype=jnp.int32)
    full_re, full_im = phase_table(all_rows, all_rows, first_len)
    columns_whole = lax.all_to_all(signal, "row", split_axis=2, concat_axis=1, tiled=True)
    pair_b_re = row_product(full_re, columns_whole)
    pair_b_im = row_product(full_im, columns_whole)
    pair_tw_re, pair_tw_im = twist_table(all_rows, pair_cols, seq_len)
    pair_mix_re = (pair_b_re * pair_tw_re - pair_b_im * pair_tw_im).astype(jnp.bfloat16)
    pair_mix_im = (pair_b_re * pair_tw_im + pair_b_im * pair_tw_re).astype(jnp.bfloat16)
    mixed_re, mixed_im = (
        lax.all_to_all(pair_mix_re, "row", split_axis=1, concat_axis=2, tiled=True),
        lax.all_to_all(pair_mix_im, "row", split_axis=1, concat_axis=2, tiled=True),
    )
    part_re = lax.all_gather(mixed_re, "col", axis=2, tiled=True)
    part_im = lax.all_gather(mixed_im, "col", axis=2, tiled=True)
    all_cols = jnp.arange(second_len, dtype=jnp.int32)
    phase_re, phase_im = phase_table(all_cols, own_cols, second_len)
    spec_re = column_product(part_re, phase_re) - column_product(part_im, phase_im)
    spec_im = column_product(part_re, phase_im) + column_product(part_im, phase_re)
    prod_re = (spec_re * filter_real - spec_im * filter_imag).astype(jnp.bfloat16)
    prod_im = (spec_re * filter_imag + spec_im * filter_real).astype(jnp.bfloat16)
    part_re = lax.all_gather(prod_re, "col", axis=2, tiled=True)
    part_im = lax.all_gather(prod_im, "col", axis=2, tiled=True)
    new_re = column_product(part_re, phase_re) + column_product(part_im, phase_im)
    new_im = column_product(part_im, phase_re) - column_product(part_re, phase_im)
    unwound_re = (new_re * twist_re + new_im * twist_im).astype(jnp.bfloat16)
    unwound_im = (new_im * twist_re - new_re * twist_im).astype(jnp.bfloat16)
    pair_un_re, pair_un_im = (
        lax.all_to_all(unwound_re, "row", split_axis=2, concat_axis=1, tiled=True),
        lax.all_to_all(unwound_im, "row", split_axis=2, concat_axis=1, tiled=True),
    )
    pair_total = row_product(full_re, pair_un_re) + row_product(full_im, pair_un_im)
    pair_out = (
        pair_total / seq_len + skip[:, None, None] * columns_whole.astype(jnp.float32)
    ).astype(jnp.bfloat16)
    return lax.all_to_all(pair_out, "row", split_axis=1, concat_axis=2, tiled=True)


def numpy_phase(left_ids, right_ids, modulus):
    product = (left_ids[:, None].astype(np.int64) * right_ids[None, :]) % modulus
    angle = np.float32(-2.0 * math.pi / modulus) * product.astype(np.float32)
    return np.cos(angle), np.sin(angle)


def tables(first_len, second_len, row_count, parts):
    height = row_count // parts
    half = row_count // 2
    rows = np.arange(first_len)
    cols = np.arange(second_len)
    blocks = rows.reshape(-1, row_count)
    first_re, first_im = numpy_phase(rows, rows, first_len)
    twist_re, twist_im = numpy_phase(rows, cols, first_len * second_len)
    first, twist, inverse = [], [], []
    for part in range(parts):
        own, other = (blocks[:, p * height : (p + 1) * height].reshape(-1) for p in (part, part ^ 1))
        near, far = (blocks[:, h * half : (h + 1) * half].reshape(-1) for h in (part % 2, 1 - part % 2))
        order = np.concatenate([near, far])
        first.append(np.concatenate([first_re[np.ix_(own, order)], first_im[np.ix_(own, order)]]))
        twist.append(np.concatenate([twist_re[own], twist_im[own]]))
        inverse.append(
            np.concatenate([t[np.ix_(near, ids)] for ids in (own, other) for t in (first_re, first_im)], axis=1)
        )
    second = np.concatenate(numpy_phase(cols, cols, second_len), axis=1)
    return (
        jnp.asarray(np.stack(first), jnp.bfloat16),
        jnp.asarray(np.stack(twist), jnp.float32),
        jnp.asarray(np.stack(inverse), jnp.bfloat16),
        jnp.asarray(second, jnp.bfloat16),
    )


def dot(left, right):
    return jnp.dot(left, right, preferred_element_type=jnp.float32)


def pack_kernel(signal_ref, real_ref, imag_ref, send_ref, sems):
    rows, parts, _, _ = send_ref.shape
    row_count, col_count = signal_ref.shape[-2:]
    half = row_count // 2
    height = row_count // parts
    copies = []
    for part in range(parts):
        start = part % 2 * half
        copies.append((signal_ref.at[:, start : start + half], send_ref.at[:, part, :half]))
        cut = slice(part * height, (part + 1) * height)
        copies.append((real_ref.at[:, cut], send_ref.at[:, part, half : half + height]))
        copies.append((imag_ref.at[:, cut], send_ref.at[:, part, half + height :]))
    copies = [pltpu.make_async_copy(a, b, sems.at[i]) for i, (a, b) in enumerate(copies)]
    for copy in copies:
        copy.start()
    for copy in copies:
        copy.wait()


def spectrum_kernel(got_ref, swapped_ref, first_ref, twist_ref, second_ref, out_ref):
    rows, parts, _, col_count = got_ref.shape
    second_len = parts * col_count
    half = first_ref.shape[1] // 2 // rows
    mine = first_ref.shape[0] // 2
    height = mine // rows
    twist_re = twist_ref[:mine]
    twist_im = twist_ref[mine:]

    def columns(ref, start, count, kind):
        return jnp.concatenate(
            [
                ref[:, part, start : start + count, :].astype(kind).reshape(rows * count, col_count)
                for part in range(parts)
            ],
            axis=1,
        )

    series = jnp.concatenate(
        [columns(got_ref, 0, half, jnp.bfloat16), columns(swapped_ref, 0, half, jnp.bfloat16)], axis=0
    )
    both = dot(first_ref[...], series)
    half_re, half_im = both[:mine], both[mine:]
    mixed = jnp.concatenate(
        [half_re * twist_re - half_im * twist_im, half_re * twist_im + half_im * twist_re], axis=0
    ).astype(jnp.bfloat16)
    both = dot(mixed, second_ref[...])
    spec_re = both[:mine, :second_len] - both[mine:, second_len:]
    spec_im = both[:mine, second_len:] + both[mine:, :second_len]
    filt_re = columns(got_ref, half, height, jnp.float32)
    filt_im = columns(got_ref, half + height, height, jnp.float32)
    prod = jnp.concatenate(
        [spec_re * filt_re - spec_im * filt_im, spec_re * filt_im + spec_im * filt_re], axis=0
    ).astype(jnp.bfloat16)
    both = dot(prod, second_ref[...])
    back_re = both[:mine, :second_len] + both[mine:, second_len:]
    back_im = both[mine:, :second_len] - both[:mine, second_len:]
    out_ref[...] = jnp.concatenate(
        [back_re * twist_re + back_im * twist_im, back_im * twist_re - back_re * twist_im], axis=0
    ).astype(jnp.bfloat16)


def inverse_kernel(skips_ref, own_ref, other_ref, inverse_ref, got_ref, out_ref):
    rows, parts, half, col_count = out_ref.shape
    seq_len = rows * half * 2 * parts * col_count
    both = jnp.concatenate([own_ref[...], other_ref[...]], axis=0)
    total = dot(inverse_ref[...], both) / seq_len
    for part in range(parts):
        piece = total[:, part * col_count : (part + 1) * col_count].reshape(rows, half, col_count)
        series = got_ref[:, part, :half, :].astype(jnp.float32)
        out_ref[:, part] = (piece + skips_ref[part] * series).astype(jnp.bfloat16)


def in_vmem(array):
    return pltpu.with_memory_space_constraint(array, pltpu.VMEM)


def call(kernel, out_shape, *args, **options):
    return pl.pallas_call(
        kernel,
        out_shape=pltpu.VMEM(out_shape, jnp.bfloat16),
        in_specs=[pl.BlockSpec(memory_space=pltpu.VMEM)] * len(args),
        out_specs=pl.BlockSpec(memory_space=pltpu.VMEM),
        **options,
    )(*map(in_vmem, args))


def local_by_channels(signal, filter_real, filter_imag, skip):
    channels, row_count, col_count = signal.shape
    rows = lax.axis_size("row")
    parts = lax.axis_size("col")
    share = channels // rows
    half = row_count // 2
    tall = half + 2 * (row_count // parts)
    every = ("row", "col")
    pairs = [(part, part ^ 1) for part in range(parts)]
    part = lax.axis_index("col")
    first, twist, inverse, second = tables(rows * row_count, parts * col_count, row_count, parts)
    first, twist, inverse = (lax.dynamic_index_in_dim(t, part, 0, keepdims=False) for t in (first, twist, inverse))
    outs = []
    for turn in range(share):
        own = slice(turn * rows, (turn + 1) * rows)
        send = pl.pallas_call(
            pack_kernel,
            out_shape=pltpu.VMEM((rows, parts, tall, col_count), jnp.bfloat16),
            in_specs=[pl.BlockSpec(memory_space=pl.ANY)] * 3,
            out_specs=pl.BlockSpec(memory_space=pltpu.VMEM),
            scratch_shapes=[pltpu.SemaphoreType.DMA((3 * parts,))],
        )(signal[own], filter_real[own], filter_imag[own])
        got = lax.all_to_all(send.reshape(rows * parts, tall, col_count), every, 0, 0, tiled=True)
        got = got.reshape(rows, parts, tall, col_count)
        swapped = lax.ppermute(got, "col", pairs)
        unwound = call(
            spectrum_kernel, first.shape[:1] + (parts * col_count,), got, swapped, first, twist, second
        )
        other = lax.ppermute(unwound, "col", pairs)
        skips = jnp.where(jnp.arange(parts) // 2 == part // 2, skip[turn * rows + lax.axis_index("row")], 0.0)
        partial_sums = pl.pallas_call(
            inverse_kernel,
            out_shape=pltpu.VMEM((rows, parts, half, col_count), jnp.bfloat16),
            in_specs=[pl.BlockSpec(memory_space=pltpu.SMEM)] + [pl.BlockSpec(memory_space=pltpu.VMEM)] * 4,
            out_specs=pl.BlockSpec(memory_space=pltpu.VMEM),
        )(skips, *map(in_vmem, (unwound, other, inverse, got)))
        back = lax.all_to_all(partial_sums.reshape(rows * parts, half, col_count), every, 0, 0, tiled=True)
        back = back.reshape(rows, parts // 2, row_count, col_count)
        outs.append(jnp.sum(back.astype(jnp.float32), axis=1).astype(jnp.bfloat16))
    return outs[0] if share == 1 else jnp.concatenate(outs, axis=0)


def local(signal, filter_real, filter_imag, skip):
    channels, row_count, _ = signal.shape
    parts = lax.axis_size("col")
    if channels % lax.axis_size("row") == 0 and parts % 2 == 0 and row_count % (8 * parts) == 0:
        return local_by_channels(signal, filter_real, filter_imag, skip)
    return local_by_columns(signal, filter_real, filter_imag, skip)


def solution(mesh):
    in_specs = (P(None, "row", "col"), P(None, "row", "col"), P(None, "row", "col"), P())
    out_specs = P(None, "row", "col")
    return jax.shard_map(local, mesh=mesh, in_specs=in_specs, out_specs=out_specs, check_vma=False)
```

```python
import functools
import math

import jax
import jax.numpy as jnp
import numpy as np
from jax import lax
from jax.experimental import pallas as pl
from jax.experimental.pallas import tpu as pltpu
from jax.sharding import PartitionSpec as P


def phase_table(left_ids, right_ids, modulus):
    product = left_ids[:, None] * right_ids[None, :] % modulus
    angle = -2.0 * math.pi / modulus * product.astype(jnp.float32)
    return (jnp.cos(angle).astype(jnp.bfloat16), jnp.sin(angle).astype(jnp.bfloat16))


def twist_table(left_ids, right_ids, modulus):
    product = left_ids[:, None] * right_ids[None, :] % modulus
    angle = -2.0 * math.pi / modulus * product.astype(jnp.float32)
    return (jnp.cos(angle), jnp.sin(angle))


def column_product(series, phase):
    return jnp.einsum("crn,nk->crk", series, phase, preferred_element_type=jnp.float32)


def row_product(phase, series):
    return jnp.einsum("rn,cnj->crj", phase, series, preferred_element_type=jnp.float32)


def local_by_columns(signal, filter_real, filter_imag, skip):
    channels, row_count, col_count = signal.shape
    first_len = row_count * lax.axis_size("row")
    second_len = col_count * lax.axis_size("col")
    seq_len = first_len * second_len
    row_offset = lax.axis_index("row") * row_count
    col_offset = lax.axis_index("col") * col_count
    own_rows = row_offset + jnp.arange(row_count, dtype=jnp.int32)
    own_cols = col_offset + jnp.arange(col_count, dtype=jnp.int32)
    twist_re, twist_im = twist_table(own_rows, own_cols, seq_len)
    pair_width = col_count // lax.axis_size("row")
    pair_cols = (
        col_offset + lax.axis_index("row") * pair_width + jnp.arange(pair_width, dtype=jnp.int32)
    )
    all_rows = jnp.arange(first_len, dtype=jnp.int32)
    full_re, full_im = phase_table(all_rows, all_rows, first_len)
    columns_whole = lax.all_to_all(signal, "row", split_axis=2, concat_axis=1, tiled=True)
    pair_b_re = row_product(full_re, columns_whole)
    pair_b_im = row_product(full_im, columns_whole)
    pair_tw_re, pair_tw_im = twist_table(all_rows, pair_cols, seq_len)
    pair_mix_re = (pair_b_re * pair_tw_re - pair_b_im * pair_tw_im).astype(jnp.bfloat16)
    pair_mix_im = (pair_b_re * pair_tw_im + pair_b_im * pair_tw_re).astype(jnp.bfloat16)
    mixed_re, mixed_im = (
        lax.all_to_all(pair_mix_re, "row", split_axis=1, concat_axis=2, tiled=True),
        lax.all_to_all(pair_mix_im, "row", split_axis=1, concat_axis=2, tiled=True),
    )
    part_re = lax.all_gather(mixed_re, "col", axis=2, tiled=True)
    part_im = lax.all_gather(mixed_im, "col", axis=2, tiled=True)
    all_cols = jnp.arange(second_len, dtype=jnp.int32)
    phase_re, phase_im = phase_table(all_cols, own_cols, second_len)
    spec_re = column_product(part_re, phase_re) - column_product(part_im, phase_im)
    spec_im = column_product(part_re, phase_im) + column_product(part_im, phase_re)
    prod_re = (spec_re * filter_real - spec_im * filter_imag).astype(jnp.bfloat16)
    prod_im = (spec_re * filter_imag + spec_im * filter_real).astype(jnp.bfloat16)
    part_re = lax.all_gather(prod_re, "col", axis=2, tiled=True)
    part_im = lax.all_gather(prod_im, "col", axis=2, tiled=True)
    new_re = column_product(part_re, phase_re) + column_product(part_im, phase_im)
    new_im = column_product(part_im, phase_re) - column_product(part_re, phase_im)
    unwound_re = (new_re * twist_re + new_im * twist_im).astype(jnp.bfloat16)
    unwound_im = (new_im * twist_re - new_re * twist_im).astype(jnp.bfloat16)
    pair_un_re, pair_un_im = (
        lax.all_to_all(unwound_re, "row", split_axis=2, concat_axis=1, tiled=True),
        lax.all_to_all(unwound_im, "row", split_axis=2, concat_axis=1, tiled=True),
    )
    pair_total = row_product(full_re, pair_un_re) + row_product(full_im, pair_un_im)
    pair_out = (
        pair_total / seq_len + skip[:, None, None] * columns_whole.astype(jnp.float32)
    ).astype(jnp.bfloat16)
    return lax.all_to_all(pair_out, "row", split_axis=1, concat_axis=2, tiled=True)


def numpy_phase(left_ids, right_ids, modulus):
    product = (left_ids[:, None].astype(np.int64) * right_ids[None, :]) % modulus
    angle = np.float32(-2.0 * math.pi / modulus) * product.astype(np.float32)
    return np.cos(angle), np.sin(angle)


def tables(first_len, second_len, row_count, parts):
    height = row_count // parts
    half = row_count // 2
    rows = np.arange(first_len)
    cols = np.arange(second_len)
    blocks = rows.reshape(-1, row_count)
    first_re, first_im = numpy_phase(rows, rows, first_len)
    first, inverse = [], []
    for part in range(parts):
        own, other = (blocks[:, p * height : (p + 1) * height].reshape(-1) for p in (part, part ^ 1))
        near, far = (blocks[:, h * half : (h + 1) * half].reshape(-1) for h in (part % 2, 1 - part % 2))
        order = np.concatenate([near, far])
        first.append(np.concatenate([first_re[np.ix_(own, order)], first_im[np.ix_(own, order)]]))
        inverse.append(
            np.concatenate([t[np.ix_(near, ids)] for ids in (own, other) for t in (first_re, first_im)], axis=1)
        )
    block_twist = np.stack(numpy_phase(blocks[:, 0], cols, first_len * second_len))
    row_twist = np.stack(numpy_phase(blocks[0], cols, first_len * second_len))
    row_twist = row_twist.reshape(2, parts, height, second_len).swapaxes(0, 1)
    second = np.concatenate(numpy_phase(cols, cols, second_len), axis=1)
    return (
        jnp.asarray(np.stack(first), jnp.bfloat16),
        jnp.asarray(block_twist, jnp.float32),
        jnp.asarray(row_twist, jnp.float32),
        jnp.asarray(np.stack(inverse), jnp.bfloat16),
        jnp.asarray(second, jnp.bfloat16),
    )


def dot(left, right):
    return jnp.dot(left, right, preferred_element_type=jnp.float32)


def pack_kernel(signal_ref, real_ref, imag_ref, send_ref, sems):
    rows, parts, _, _ = send_ref.shape
    row_count, col_count = signal_ref.shape[-2:]
    half = row_count // 2
    height = row_count // parts
    copies = []
    for part in range(parts):
        start = part % 2 * half
        copies.append((signal_ref.at[:, start : start + half], send_ref.at[:, part, :half]))
        cut = slice(part * height, (part + 1) * height)
        copies.append((real_ref.at[:, cut], send_ref.at[:, part, half : half + height]))
        copies.append((imag_ref.at[:, cut], send_ref.at[:, part, half + height :]))
    copies = [pltpu.make_async_copy(a, b, sems.at[i]) for i, (a, b) in enumerate(copies)]
    for copy in copies:
        copy.start()
    for copy in copies:
        copy.wait()


def columns(ref, start, count, kind):
    rows, parts, _, col_count = ref.shape
    return jnp.concatenate(
        [ref[:, part, start : start + count, :].astype(kind).reshape(rows * count, col_count) for part in range(parts)],
        axis=1,
    )


def near_kernel(got_ref, first_ref, out_ref):
    count = first_ref.shape[2] // 2
    series = columns(got_ref, 0, count // got_ref.shape[0], jnp.bfloat16)
    out_ref[...] = dot(first_ref[lax.axis_index("col"), :, :count], series)


def spectrum_kernel(near_ref, got_ref, swapped_ref, first_ref, block_ref, row_ref, second_ref, out_ref):
    rows, parts, _, col_count = got_ref.shape
    second_len = parts * col_count
    count = first_ref.shape[2] // 2
    half = count // rows
    mine = first_ref.shape[1] // 2
    height = mine // rows
    part = lax.axis_index("col")
    block_re, block_im = block_ref[0][:, None, :], block_ref[1][:, None, :]
    row_re, row_im = row_ref[part, 0][None], row_ref[part, 1][None]
    twist_re = (block_re * row_re - block_im * row_im).reshape(mine, second_len)
    twist_im = (block_re * row_im + block_im * row_re).reshape(mine, second_len)

    both = near_ref[...] + dot(first_ref[part, :, count:], columns(swapped_ref, 0, half, jnp.bfloat16))
    half_re, half_im = both[:mine], both[mine:]
    mixed = jnp.concatenate(
        [half_re * twist_re - half_im * twist_im, half_re * twist_im + half_im * twist_re], axis=0
    ).astype(jnp.bfloat16)
    both = dot(mixed, second_ref[...])
    spec_re = both[:mine, :second_len] - both[mine:, second_len:]
    spec_im = both[:mine, second_len:] + both[mine:, :second_len]
    filt_re = columns(got_ref, half, height, jnp.float32)
    filt_im = columns(got_ref, half + height, height, jnp.float32)
    prod = jnp.concatenate(
        [spec_re * filt_re - spec_im * filt_im, spec_re * filt_im + spec_im * filt_re], axis=0
    ).astype(jnp.bfloat16)
    both = dot(prod, second_ref[...])
    back_re = both[:mine, :second_len] + both[mine:, second_len:]
    back_im = both[mine:, :second_len] - both[:mine, second_len:]
    out_ref[...] = jnp.concatenate(
        [back_re * twist_re + back_im * twist_im, back_im * twist_re - back_re * twist_im], axis=0
    ).astype(jnp.bfloat16)


def inverse_kernel(own_ref, other_ref, inverse_ref, got_ref, skip_ref, out_ref, *, turn):
    rows, parts, half, col_count = out_ref.shape
    seq_len = rows * half * 2 * parts * col_count
    mine = lax.axis_index("col")
    channel = turn * rows + lax.axis_index("row")
    at = lax.broadcasted_iota(jnp.int32, skip_ref.shape, 1)
    skip = jnp.sum(jnp.where(at == channel, skip_ref[...], 0.0), axis=1, keepdims=True)
    both = jnp.concatenate([own_ref[...], other_ref[...]], axis=0)
    total = dot(inverse_ref[mine], both) / seq_len
    for part in range(parts):
        piece = total[:, part * col_count : (part + 1) * col_count]
        series = got_ref[:, part, :half, :].astype(jnp.float32).reshape(rows * half, col_count)
        term = jnp.where(mine // 2 == part // 2, skip, 0.0) * series
        out_ref[:, part] = (piece + term).astype(jnp.bfloat16).reshape(rows, half, col_count)


def call(kernel, out_shape, *args, kind=jnp.bfloat16, flops=None):
    return pl.pallas_call(
        kernel,
        out_shape=pltpu.VMEM(out_shape, kind),
        in_specs=[pl.BlockSpec(memory_space=pltpu.VMEM)] * len(args),
        out_specs=pl.BlockSpec(memory_space=pltpu.VMEM),
        cost_estimate=flops and pl.CostEstimate(flops=flops, bytes_accessed=0, transcendentals=0),
    )(*(pltpu.with_memory_space_constraint(arg, pltpu.VMEM) for arg in args))


def local_by_channels(signal, filter_real, filter_imag, skip):
    channels, row_count, col_count = signal.shape
    rows = lax.axis_size("row")
    parts = lax.axis_size("col")
    share = channels // rows
    half = row_count // 2
    tall = half + 2 * (row_count // parts)
    every = ("row", "col")
    pairs = [(part, part ^ 1) for part in range(parts)]
    first, block, row, inverse, second = tables(rows * row_count, parts * col_count, row_count, parts)
    outs = []
    for turn in range(share):
        own = slice(turn * rows, (turn + 1) * rows)
        send = pl.pallas_call(
            pack_kernel,
            out_shape=pltpu.VMEM((rows, parts, tall, col_count), jnp.bfloat16),
            in_specs=[pl.BlockSpec(memory_space=pl.ANY)] * 3,
            out_specs=pl.BlockSpec(memory_space=pltpu.VMEM),
            scratch_shapes=[pltpu.SemaphoreType.DMA((3 * parts,))],
        )(signal[own], filter_real[own], filter_imag[own])
        got = lax.all_to_all(send.reshape(rows * parts, tall, col_count), every, 0, 0, tiled=True)
        got = got.reshape(rows, parts, tall, col_count)
        swapped = lax.ppermute(got, "col", pairs)
        shape = (first.shape[1], parts * col_count)
        near = call(near_kernel, shape, got, first, kind=jnp.float32, flops=10**9)
        unwound = call(spectrum_kernel, shape, near, got, swapped, first, block, row, second)
        other = lax.ppermute(unwound, "col", pairs)
        partial_sums = call(
            functools.partial(inverse_kernel, turn=turn),
            (rows, parts, half, col_count),
            unwound,
            other,
            inverse,
            got,
            skip[None],
        )
        back = lax.all_to_all(partial_sums.reshape(rows * parts, half, col_count), every, 0, 0, tiled=True)
        back = back.reshape(rows, parts // 2, row_count, col_count)
        outs.append(jnp.sum(back.astype(jnp.float32), axis=1).astype(jnp.bfloat16))
    return outs[0] if share == 1 else jnp.concatenate(outs, axis=0)


def local(signal, filter_real, filter_imag, skip):
    channels, row_count, _ = signal.shape
    parts = lax.axis_size("col")
    if channels % lax.axis_size("row") == 0 and parts % 2 == 0 and row_count % (8 * parts) == 0:
        return local_by_channels(signal, filter_real, filter_imag, skip)
    return local_by_columns(signal, filter_real, filter_imag, skip)


def solution(mesh):
    in_specs = (P(None, "row", "col"), P(None, "row", "col"), P(None, "row", "col"), P())
    out_specs = P(None, "row", "col")
    return jax.shard_map(local, mesh=mesh, in_specs=in_specs, out_specs=out_specs, check_vma=False)
```

```python
import functools
import math

import jax
import jax.numpy as jnp
import numpy as np
from jax import lax
from jax.experimental import pallas as pl
from jax.experimental.pallas import tpu as pltpu
from jax.sharding import PartitionSpec as P


def phase_table(left_ids, right_ids, modulus):
    product = left_ids[:, None] * right_ids[None, :] % modulus
    angle = -2.0 * math.pi / modulus * product.astype(jnp.float32)
    return (jnp.cos(angle).astype(jnp.bfloat16), jnp.sin(angle).astype(jnp.bfloat16))


def twist_table(left_ids, right_ids, modulus):
    product = left_ids[:, None] * right_ids[None, :] % modulus
    angle = -2.0 * math.pi / modulus * product.astype(jnp.float32)
    return (jnp.cos(angle), jnp.sin(angle))


def column_product(series, phase):
    return jnp.einsum("crn,nk->crk", series, phase, preferred_element_type=jnp.float32)


def row_product(phase, series):
    return jnp.einsum("rn,cnj->crj", phase, series, preferred_element_type=jnp.float32)


def local_by_columns(signal, filter_real, filter_imag, skip):
    channels, row_count, col_count = signal.shape
    first_len = row_count * lax.axis_size("row")
    second_len = col_count * lax.axis_size("col")
    seq_len = first_len * second_len
    row_offset = lax.axis_index("row") * row_count
    col_offset = lax.axis_index("col") * col_count
    own_rows = row_offset + jnp.arange(row_count, dtype=jnp.int32)
    own_cols = col_offset + jnp.arange(col_count, dtype=jnp.int32)
    twist_re, twist_im = twist_table(own_rows, own_cols, seq_len)
    pair_width = col_count // lax.axis_size("row")
    pair_cols = (
        col_offset + lax.axis_index("row") * pair_width + jnp.arange(pair_width, dtype=jnp.int32)
    )
    all_rows = jnp.arange(first_len, dtype=jnp.int32)
    full_re, full_im = phase_table(all_rows, all_rows, first_len)
    columns_whole = lax.all_to_all(signal, "row", split_axis=2, concat_axis=1, tiled=True)
    pair_b_re = row_product(full_re, columns_whole)
    pair_b_im = row_product(full_im, columns_whole)
    pair_tw_re, pair_tw_im = twist_table(all_rows, pair_cols, seq_len)
    pair_mix_re = (pair_b_re * pair_tw_re - pair_b_im * pair_tw_im).astype(jnp.bfloat16)
    pair_mix_im = (pair_b_re * pair_tw_im + pair_b_im * pair_tw_re).astype(jnp.bfloat16)
    mixed_re, mixed_im = (
        lax.all_to_all(pair_mix_re, "row", split_axis=1, concat_axis=2, tiled=True),
        lax.all_to_all(pair_mix_im, "row", split_axis=1, concat_axis=2, tiled=True),
    )
    part_re = lax.all_gather(mixed_re, "col", axis=2, tiled=True)
    part_im = lax.all_gather(mixed_im, "col", axis=2, tiled=True)
    all_cols = jnp.arange(second_len, dtype=jnp.int32)
    phase_re, phase_im = phase_table(all_cols, own_cols, second_len)
    spec_re = column_product(part_re, phase_re) - column_product(part_im, phase_im)
    spec_im = column_product(part_re, phase_im) + column_product(part_im, phase_re)
    prod_re = (spec_re * filter_real - spec_im * filter_imag).astype(jnp.bfloat16)
    prod_im = (spec_re * filter_imag + spec_im * filter_real).astype(jnp.bfloat16)
    part_re = lax.all_gather(prod_re, "col", axis=2, tiled=True)
    part_im = lax.all_gather(prod_im, "col", axis=2, tiled=True)
    new_re = column_product(part_re, phase_re) + column_product(part_im, phase_im)
    new_im = column_product(part_im, phase_re) - column_product(part_re, phase_im)
    unwound_re = (new_re * twist_re + new_im * twist_im).astype(jnp.bfloat16)
    unwound_im = (new_im * twist_re - new_re * twist_im).astype(jnp.bfloat16)
    pair_un_re, pair_un_im = (
        lax.all_to_all(unwound_re, "row", split_axis=2, concat_axis=1, tiled=True),
        lax.all_to_all(unwound_im, "row", split_axis=2, concat_axis=1, tiled=True),
    )
    pair_total = row_product(full_re, pair_un_re) + row_product(full_im, pair_un_im)
    pair_out = (
        pair_total / seq_len + skip[:, None, None] * columns_whole.astype(jnp.float32)
    ).astype(jnp.bfloat16)
    return lax.all_to_all(pair_out, "row", split_axis=1, concat_axis=2, tiled=True)


def numpy_phase(left_ids, right_ids, modulus):
    product = (left_ids[:, None].astype(np.int64) * right_ids[None, :]) % modulus
    angle = np.float32(-2.0 * math.pi / modulus) * product.astype(np.float32)
    return np.cos(angle), np.sin(angle)


def tables(first_len, second_len, row_count, parts):
    height = row_count // parts
    rows = np.arange(first_len)
    cols = np.arange(second_len)
    by_core = cols.reshape(parts, 2, -1).swapaxes(0, 1).reshape(-1)
    blocks = rows.reshape(-1, row_count)
    own = [blocks[:, part * height : (part + 1) * height].reshape(-1) for part in range(parts)]
    first = np.stack(numpy_phase(rows, rows, first_len))
    sides = [[[kind[own[2 * side + core]] for core in range(2)] for kind in first] for side in range(parts // 2)]
    inverse = [
        np.concatenate([kind[:, own[member]] for kind in first for member in (part, part ^ 1)], axis=1)
        for part in range(parts)
    ]
    block_twist = numpy_phase(blocks[:, 0], by_core, first_len * second_len)
    row_twist = numpy_phase(blocks[0], by_core, first_len * second_len)
    forward = np.concatenate(numpy_phase(by_core, cols, second_len), axis=1)
    backward = np.concatenate(numpy_phase(cols, by_core, second_len), axis=1)
    return (
        jnp.asarray(np.array(sides), jnp.bfloat16),
        jnp.asarray(np.stack(block_twist), jnp.float32),
        jnp.asarray(np.stack(row_twist), jnp.float32),
        jnp.asarray(np.stack(inverse), jnp.bfloat16),
        jnp.asarray(forward, jnp.bfloat16),
        jnp.asarray(backward, jnp.bfloat16),
    )


def dot(left, right):
    return jnp.dot(left, right, preferred_element_type=jnp.float32)


def crossed(one, two):
    half = one.shape[-1] // 2
    return (
        jnp.concatenate([one[..., :half], two[..., :half]], axis=-1),
        jnp.concatenate([one[..., half:], two[..., half:]], axis=-1),
    )


def side_and_core():
    part = lax.axis_index("col")
    return part // 2, part % 2


def half_of(core, width):
    return pl.ds(pl.multiple_of(core * width, width), width)


def series_of(ref):
    rows, parts, tall, width = ref.shape
    half = tall // 2
    strips = []
    for part in range(0, parts, 2):
        pair = crossed(ref[:, part, :half, :], ref[:, part + 1, :half, :])
        strips.append(jnp.concatenate(pair, axis=1).reshape(rows * 2 * half, width))
    return jnp.concatenate(strips, axis=1)


def filter_of(ref, start, count):
    rows, parts, _, width = ref.shape
    return jnp.concatenate(
        [ref[:, part, start : start + count, :].astype(jnp.float32).reshape(rows * count, width) for part in range(parts)],
        axis=1,
    )


def twists(block_ref, row_ref, height, side, core, span):
    block_re, block_im = block_ref[0, :, span][:, None, :], block_ref[1, :, span][:, None, :]
    shape = (block_ref.shape[1] * height, span.size)
    re, im = [], []
    for member in (core, 1 - core):
        at = pl.ds(pl.multiple_of((2 * side + member) * height, height), height)
        row_re, row_im = row_ref[0, at, span][None], row_ref[1, at, span][None]
        re.append((block_re * row_re - block_im * row_im).reshape(shape))
        im.append((block_re * row_im + block_im * row_re).reshape(shape))
    return jnp.concatenate(re, axis=0), jnp.concatenate(im, axis=0)


def turned(re, im, by_re, by_im):
    return re * by_re - im * by_im, re * by_im + im * by_re


def widened(pair):
    re, im = (each.astype(jnp.bfloat16) for each in pair)
    return jnp.concatenate([jnp.concatenate([re, -im], axis=1), jnp.concatenate([im, re], axis=1)], axis=0)


def widened_back(pair):
    re, im = (each.astype(jnp.bfloat16) for each in pair)
    return jnp.concatenate([jnp.concatenate([re, im], axis=1), jnp.concatenate([im, -re], axis=1)], axis=0)


def pack_kernel(signal_ref, real_ref, imag_ref, skip_ref, send_ref, skips_ref, signal_buf, sems):
    _, parts, _, _ = send_ref.shape
    row_count = signal_ref.shape[-2]
    half = row_count // 2
    height = row_count // parts
    copies = [(signal_ref, signal_buf), (skip_ref, skips_ref)]
    for part in range(parts):
        cut = slice(part * height, (part + 1) * height)
        copies.append((real_ref.at[:, cut], send_ref.at[:, part, half : half + height]))
        copies.append((imag_ref.at[:, cut], send_ref.at[:, part, half + height :]))
    copies = [pltpu.make_async_copy(a, b, sems.at[i]) for i, (a, b) in enumerate(copies)]
    for copy in copies:
        copy.start()
    copies[0].wait()
    halves = crossed(signal_buf[:, :half], signal_buf[:, half:])
    for part in range(parts):
        send_ref[:, part, :half] = halves[part % 2]
    for copy in copies[1:]:
        copy.wait()


def half_transform(ref, first_ref, side, core):
    left = [first_ref[side, kind, member] for kind in range(2) for member in (core, 1 - core)]
    both = dot(jnp.concatenate(left, axis=0), series_of(ref))
    mine = both.shape[0] // 2
    return both[:mine], both[mine:]


def forward_rows(forward_ref, core):
    second_len = forward_ref.shape[0]
    rows = half_of(core, second_len // 2)
    return jnp.concatenate([forward_ref[rows, :second_len], forward_ref[rows, second_len:]], axis=0)


def near_kernel(got_ref, first_ref, block_ref, row_ref, forward_ref, skip_ref, spec_ref, twist_ref, term_ref, *, turn):
    rows, parts, tall, width = got_ref.shape
    side, core = side_and_core()
    first_len, second_len = first_ref.shape[-1], forward_ref.shape[0]
    height = tall // 4
    near_len = second_len // 2
    twist = twists(block_ref, row_ref, height, side, core, half_of(core, near_len))
    mixed = turned(*half_transform(got_ref, first_ref, side, core), *twist)
    spec_ref[...] = dot(widened(mixed), forward_rows(forward_ref, core))
    twist_ref[0], twist_ref[1] = twists(block_ref, row_ref, height, side, core, half_of(1 - core, near_len))
    twist_ref[2], twist_ref[3] = (each / (first_len * second_len) for each in twist)

    at = lax.broadcasted_iota(jnp.int32, skip_ref.shape, 1)
    channel = turn * rows + lax.axis_index("row")
    skip = jnp.sum(jnp.where(at == channel, skip_ref[...], 0.0), axis=1, keepdims=True)
    series = series_of(got_ref)
    for place in range(parts // 2):
        cut = slice(place * width, (place + 1) * width)
        term_ref[:, cut] = jnp.where(side == place, skip, 0.0) * series[:, cut].astype(jnp.float32)


def spectrum_kernel(spec_ref, twist_ref, term_ref, got_ref, swapped_ref, first_ref, forward_ref, backward_ref, inverse_ref, out_ref):
    rows, parts, tall, width = got_ref.shape
    side, core = side_and_core()
    half, height = tall // 2, tall // 4
    second_len = forward_ref.shape[0]
    near_len = second_len // 2
    mixed = turned(*half_transform(swapped_ref, first_ref, side, core), twist_ref[0], twist_ref[1])
    spec = spec_ref[...] + dot(widened(mixed), forward_rows(forward_ref, 1 - core))
    mine = spec.shape[0] // 2
    filt_re, filt_im = (
        jnp.concatenate([filter_of(ref, start, height) for ref in (got_ref, swapped_ref)], axis=0)
        for start in (half, half + height)
    )
    prod = turned(spec[:mine], spec[mine:], filt_re, filt_im)
    cols = [pl.ds(pl.multiple_of(at + core * near_len, near_len), near_len) for at in (0, second_len)]
    back = dot(widened_back(prod), jnp.concatenate([backward_ref[:, col] for col in cols], axis=0))
    unwound = turned(back[:mine], back[mine:], twist_ref[2], -twist_ref[3])
    unwound = jnp.concatenate(unwound, axis=0).astype(jnp.bfloat16)
    total = (dot(inverse_ref[lax.axis_index("col")], unwound) + term_ref[...]).astype(jnp.bfloat16)
    for place in range(parts // 2):
        piece = total[:, place * width : (place + 1) * width].reshape(rows, 2 * half, width)
        out_ref[:, 2 * place], out_ref[:, 2 * place + 1] = crossed(piece[:, :half], piece[:, half:])


def finish_kernel(back_ref, out_ref):
    _, parts, half, _ = back_ref.shape
    cores = []
    for core in range(2):
        shares = [back_ref[:, part].astype(jnp.float32) for part in range(core, parts, 2)]
        cores.append(sum(shares[1:], shares[0]))
    out_ref[:, :half], out_ref[:, half:] = (each.astype(jnp.bfloat16) for each in crossed(*cores))


PARAMS = pltpu.CompilerParams(vmem_limit_bytes=8 * 2**20)
IN_VMEM = pl.BlockSpec(memory_space=pltpu.VMEM)


def call(kernel, outs, *args, flops=None):
    return pl.pallas_call(
        kernel,
        out_shape=[pltpu.VMEM(shape, kind) for shape, kind in outs],
        in_specs=[IN_VMEM] * len(args),
        out_specs=[IN_VMEM] * len(outs),
        compiler_params=PARAMS,
        cost_estimate=flops and pl.CostEstimate(flops=flops, bytes_accessed=0, transcendentals=0),
    )(*(pltpu.with_memory_space_constraint(arg, pltpu.VMEM) for arg in args))


def local_by_channels(signal, filter_real, filter_imag, skip):
    channels, row_count, col_count = signal.shape
    rows = lax.axis_size("row")
    parts = lax.axis_size("col")
    share = channels // rows
    half = row_count // 2
    pairs = [(part, part ^ 1) for part in range(parts)]
    first, block, row, inverse, forward, backward = tables(rows * row_count, parts * col_count, row_count, parts)
    near_len = parts * col_count // 2
    mine = rows * row_count // (parts // 2)
    outs = []

    def exchange(array):
        flat = array.reshape((rows * parts,) + array.shape[2:])
        return lax.all_to_all(flat, ("row", "col"), 0, 0, tiled=True).reshape(array.shape)

    for turn in range(share):
        own = slice(turn * rows, (turn + 1) * rows)
        tall = half + 2 * (row_count // parts)
        args = (signal[own], filter_real[own], filter_imag[own], skip[None])
        send, skips = pl.pallas_call(
            pack_kernel,
            out_shape=[pltpu.VMEM((rows, parts, tall, col_count), jnp.bfloat16), pltpu.VMEM((1, channels), jnp.float32)],
            in_specs=[pl.BlockSpec(memory_space=pltpu.HBM)] * len(args),
            out_specs=[IN_VMEM] * 2,
            scratch_shapes=[
                pltpu.VMEM((rows, row_count, col_count), jnp.bfloat16),
                pltpu.SemaphoreType.DMA((2 * parts + 2,)),
            ],
            compiler_params=PARAMS,
            cost_estimate=pl.CostEstimate(flops=10**9, bytes_accessed=0, transcendentals=0),
        )(*(pltpu.with_memory_space_constraint(arg, pltpu.HBM) for arg in args))
        got = exchange(send)
        swapped = lax.ppermute(got, "col", pairs)
        near = call(
            functools.partial(near_kernel, turn=turn),
            [
                ((2 * mine, 2 * near_len), jnp.float32),
                ((4, mine, near_len), jnp.float32),
                ((rows * row_count, near_len), jnp.float32),
            ],
            *(got, first, block, row, forward, skips),
            flops=10**9,
        )
        (partial_sums,) = call(
            spectrum_kernel,
            [((rows, parts, half, col_count), jnp.bfloat16)],
            *(*near, got, swapped, first, forward, backward, inverse),
        )
        back = exchange(partial_sums)
        outs.append(
            pl.pallas_call(
                finish_kernel,
                out_shape=jax.ShapeDtypeStruct((rows, row_count, col_count), jnp.bfloat16),
                in_specs=[IN_VMEM],
                compiler_params=PARAMS,
            )(pltpu.with_memory_space_constraint(back, pltpu.VMEM))
        )
    return outs[0] if share == 1 else jnp.concatenate(outs, axis=0)


def local(signal, filter_real, filter_imag, skip):
    channels, row_count, col_count = signal.shape
    parts = lax.axis_size("col")
    fits = parts % 2 == 0 and row_count == 8 * parts and col_count % 128 == 0
    if channels % lax.axis_size("row") == 0 and fits:
        return local_by_channels(signal, filter_real, filter_imag, skip)
    return local_by_columns(signal, filter_real, filter_imag, skip)


def solution(mesh):
    in_specs = (P(None, "row", "col"), P(None, "row", "col"), P(None, "row", "col"), P())
    out_specs = P(None, "row", "col")
    return jax.shard_map(local, mesh=mesh, in_specs=in_specs, out_specs=out_specs, check_vma=False)
```

```python
import functools
import math

import jax
import jax.numpy as jnp
import numpy as np
from jax import lax
from jax.experimental import pallas as pl
from jax.experimental.pallas import tpu as pltpu
from jax.sharding import PartitionSpec as P


def phase_table(left_ids, right_ids, modulus):
    product = left_ids[:, None] * right_ids[None, :] % modulus
    angle = -2.0 * math.pi / modulus * product.astype(jnp.float32)
    return (jnp.cos(angle).astype(jnp.bfloat16), jnp.sin(angle).astype(jnp.bfloat16))


def twist_table(left_ids, right_ids, modulus):
    product = left_ids[:, None] * right_ids[None, :] % modulus
    angle = -2.0 * math.pi / modulus * product.astype(jnp.float32)
    return (jnp.cos(angle), jnp.sin(angle))


def column_product(series, phase):
    return jnp.einsum("crn,nk->crk", series, phase, preferred_element_type=jnp.float32)


def row_product(phase, series):
    return jnp.einsum("rn,cnj->crj", phase, series, preferred_element_type=jnp.float32)


def local_by_columns(signal, filter_real, filter_imag, skip):
    channels, row_count, col_count = signal.shape
    first_len = row_count * lax.axis_size("row")
    second_len = col_count * lax.axis_size("col")
    seq_len = first_len * second_len
    row_offset = lax.axis_index("row") * row_count
    col_offset = lax.axis_index("col") * col_count
    own_rows = row_offset + jnp.arange(row_count, dtype=jnp.int32)
    own_cols = col_offset + jnp.arange(col_count, dtype=jnp.int32)
    twist_re, twist_im = twist_table(own_rows, own_cols, seq_len)
    pair_width = col_count // lax.axis_size("row")
    pair_cols = (
        col_offset + lax.axis_index("row") * pair_width + jnp.arange(pair_width, dtype=jnp.int32)
    )
    all_rows = jnp.arange(first_len, dtype=jnp.int32)
    full_re, full_im = phase_table(all_rows, all_rows, first_len)
    columns_whole = lax.all_to_all(signal, "row", split_axis=2, concat_axis=1, tiled=True)
    pair_b_re = row_product(full_re, columns_whole)
    pair_b_im = row_product(full_im, columns_whole)
    pair_tw_re, pair_tw_im = twist_table(all_rows, pair_cols, seq_len)
    pair_mix_re = (pair_b_re * pair_tw_re - pair_b_im * pair_tw_im).astype(jnp.bfloat16)
    pair_mix_im = (pair_b_re * pair_tw_im + pair_b_im * pair_tw_re).astype(jnp.bfloat16)
    mixed_re, mixed_im = (
        lax.all_to_all(pair_mix_re, "row", split_axis=1, concat_axis=2, tiled=True),
        lax.all_to_all(pair_mix_im, "row", split_axis=1, concat_axis=2, tiled=True),
    )
    part_re = lax.all_gather(mixed_re, "col", axis=2, tiled=True)
    part_im = lax.all_gather(mixed_im, "col", axis=2, tiled=True)
    all_cols = jnp.arange(second_len, dtype=jnp.int32)
    phase_re, phase_im = phase_table(all_cols, own_cols, second_len)
    spec_re = column_product(part_re, phase_re) - column_product(part_im, phase_im)
    spec_im = column_product(part_re, phase_im) + column_product(part_im, phase_re)
    prod_re = (spec_re * filter_real - spec_im * filter_imag).astype(jnp.bfloat16)
    prod_im = (spec_re * filter_imag + spec_im * filter_real).astype(jnp.bfloat16)
    part_re = lax.all_gather(prod_re, "col", axis=2, tiled=True)
    part_im = lax.all_gather(prod_im, "col", axis=2, tiled=True)
    new_re = column_product(part_re, phase_re) + column_product(part_im, phase_im)
    new_im = column_product(part_im, phase_re) - column_product(part_re, phase_im)
    unwound_re = (new_re * twist_re + new_im * twist_im).astype(jnp.bfloat16)
    unwound_im = (new_im * twist_re - new_re * twist_im).astype(jnp.bfloat16)
    pair_un_re, pair_un_im = (
        lax.all_to_all(unwound_re, "row", split_axis=2, concat_axis=1, tiled=True),
        lax.all_to_all(unwound_im, "row", split_axis=2, concat_axis=1, tiled=True),
    )
    pair_total = row_product(full_re, pair_un_re) + row_product(full_im, pair_un_im)
    pair_out = (
        pair_total / seq_len + skip[:, None, None] * columns_whole.astype(jnp.float32)
    ).astype(jnp.bfloat16)
    return lax.all_to_all(pair_out, "row", split_axis=1, concat_axis=2, tiled=True)


def row_group(side, member, parts):
    return side + member * (parts - 1 - 2 * side)


def numpy_phase(left_ids, right_ids, modulus):
    product = (left_ids[:, None].astype(np.int64) * right_ids[None, :]) % modulus
    angle = np.float32(-2.0 * math.pi / modulus) * product.astype(np.float32)
    return np.cos(angle), np.sin(angle)


def tables(first_len, second_len, row_count, parts):
    height = row_count // parts
    rows = np.arange(first_len)
    cols = np.arange(second_len)
    by_core = cols.reshape(parts, 2, -1).swapaxes(0, 1).reshape(-1)
    blocks = rows.reshape(-1, row_count)
    groups = [row_group(part // 2, part % 2, parts) for part in range(parts)]
    own = [blocks[:, group * height : (group + 1) * height].reshape(-1) for group in groups]
    first = np.stack(numpy_phase(rows, rows, first_len))
    sides = [[[kind[own[2 * side + core]] for core in range(2)] for kind in first] for side in range(parts // 2)]
    inverse = [
        np.concatenate([kind[:, own[member]] for kind in first for member in (part, part ^ 1)], axis=1)
        for part in range(parts)
    ]
    block_twist = numpy_phase(blocks[:, 0], by_core, first_len * second_len)
    row_twist = numpy_phase(blocks[0], by_core, first_len * second_len)
    forward = np.concatenate(numpy_phase(by_core, cols, second_len), axis=1)
    backward = np.concatenate(numpy_phase(cols, by_core, second_len), axis=1)
    return (
        jnp.asarray(np.array(sides), jnp.bfloat16),
        jnp.asarray(np.stack(block_twist), jnp.float32),
        jnp.asarray(np.stack(row_twist), jnp.float32),
        jnp.asarray(np.stack(inverse), jnp.bfloat16),
        jnp.asarray(forward, jnp.bfloat16),
        jnp.asarray(backward, jnp.bfloat16),
    )


def dot(left, right):
    return jnp.dot(left, right, preferred_element_type=jnp.float32)


def crossed(one, two):
    half = one.shape[-1] // 2
    return (
        jnp.concatenate([one[..., :half], two[..., :half]], axis=-1),
        jnp.concatenate([one[..., half:], two[..., half:]], axis=-1),
    )


def side_and_core():
    part = lax.axis_index("col")
    return part // 2, part % 2


def half_of(core, width):
    return pl.ds(pl.multiple_of(core * width, width), width)


def series_of(ref):
    rows, parts, tall, width = ref.shape
    half = tall // 2
    strips = []
    for part in range(0, parts, 2):
        pair = crossed(ref[:, part, :half, :], ref[:, part + 1, :half, :])
        strips.append(jnp.concatenate(pair, axis=1).reshape(rows * 2 * half, width))
    return jnp.concatenate(strips, axis=1)


def filter_of(ref, start, count):
    rows, parts, _, width = ref.shape
    return jnp.concatenate(
        [ref[:, part, start : start + count, :].astype(jnp.float32).reshape(rows * count, width) for part in range(parts)],
        axis=1,
    )


def twists(block_ref, row_ref, height, side, core, span):
    block_re, block_im = block_ref[0, :, span][:, None, :], block_ref[1, :, span][:, None, :]
    shape = (block_ref.shape[1] * height, span.size)
    re, im = [], []
    for member in (core, 1 - core):
        group = row_group(side, member, row_ref.shape[1] // height)
        at = pl.ds(pl.multiple_of(group * height, height), height)
        row_re, row_im = row_ref[0, at, span][None], row_ref[1, at, span][None]
        re.append((block_re * row_re - block_im * row_im).reshape(shape))
        im.append((block_re * row_im + block_im * row_re).reshape(shape))
    return jnp.concatenate(re, axis=0), jnp.concatenate(im, axis=0)


def turned(re, im, by_re, by_im):
    return re * by_re - im * by_im, re * by_im + im * by_re


def widened(pair):
    re, im = (each.astype(jnp.bfloat16) for each in pair)
    return jnp.concatenate([jnp.concatenate([re, -im], axis=1), jnp.concatenate([im, re], axis=1)], axis=0)


def widened_back(pair):
    re, im = (each.astype(jnp.bfloat16) for each in pair)
    return jnp.concatenate([jnp.concatenate([re, im], axis=1), jnp.concatenate([im, -re], axis=1)], axis=0)


def pack_kernel(signal_ref, real_ref, imag_ref, skip_ref, send_ref, skips_ref, signal_buf, sems):
    _, parts, _, _ = send_ref.shape
    row_count = signal_ref.shape[-2]
    half = row_count // 2
    height = row_count // parts
    copies = [(signal_ref, signal_buf), (skip_ref, skips_ref)]
    for part in range(parts):
        group = row_group(part // 2, part % 2, parts)
        cut = slice(group * height, (group + 1) * height)
        copies.append((real_ref.at[:, cut], send_ref.at[:, part, half : half + height]))
        copies.append((imag_ref.at[:, cut], send_ref.at[:, part, half + height :]))
    copies = [pltpu.make_async_copy(a, b, sems.at[i]) for i, (a, b) in enumerate(copies)]
    for copy in copies:
        copy.start()
    copies[0].wait()
    halves = crossed(signal_buf[:, :half], signal_buf[:, half:])
    for part in range(parts):
        send_ref[:, part, :half] = halves[part % 2]
    for copy in copies[1:]:
        copy.wait()


def half_transform(ref, first_ref, side, core):
    left = [first_ref[side, kind, member] for kind in range(2) for member in (core, 1 - core)]
    both = dot(jnp.concatenate(left, axis=0), series_of(ref))
    mine = both.shape[0] // 2
    return both[:mine], both[mine:]


def forward_rows(forward_ref, core):
    second_len = forward_ref.shape[0]
    rows = half_of(core, second_len // 2)
    return jnp.concatenate([forward_ref[rows, :second_len], forward_ref[rows, second_len:]], axis=0)


def near_kernel(got_ref, first_ref, block_ref, row_ref, forward_ref, skip_ref, spec_ref, twist_ref, term_ref, *, turn):
    rows, parts, tall, width = got_ref.shape
    side, core = side_and_core()
    first_len, second_len = first_ref.shape[-1], forward_ref.shape[0]
    height = tall // 4
    near_len = second_len // 2
    twist = twists(block_ref, row_ref, height, side, core, half_of(core, near_len))
    mixed = turned(*half_transform(got_ref, first_ref, side, core), *twist)
    spec_ref[...] = dot(widened(mixed), forward_rows(forward_ref, core))
    twist_ref[0], twist_ref[1] = twists(block_ref, row_ref, height, side, core, half_of(1 - core, near_len))
    twist_ref[2], twist_ref[3] = (each / (first_len * second_len) for each in twist)

    at = lax.broadcasted_iota(jnp.int32, skip_ref.shape, 1)
    channel = turn * rows + lax.axis_index("row")
    skip = jnp.sum(jnp.where(at == channel, skip_ref[...], 0.0), axis=1, keepdims=True)
    series = series_of(got_ref)
    for place in range(parts // 2):
        cut = slice(place * width, (place + 1) * width)
        term_ref[:, cut] = jnp.where(side == place, skip, 0.0) * series[:, cut].astype(jnp.float32)


def spectrum_kernel(spec_ref, twist_ref, term_ref, got_ref, swapped_ref, first_ref, forward_ref, backward_ref, inverse_ref, out_ref):
    rows, parts, tall, width = got_ref.shape
    side, core = side_and_core()
    half, height = tall // 2, tall // 4
    second_len = forward_ref.shape[0]
    near_len = second_len // 2
    mixed = turned(*half_transform(swapped_ref, first_ref, side, core), twist_ref[0], twist_ref[1])
    spec = spec_ref[...] + dot(widened(mixed), forward_rows(forward_ref, 1 - core))
    mine = spec.shape[0] // 2
    filt_re, filt_im = (
        jnp.concatenate([filter_of(ref, start, height) for ref in (got_ref, swapped_ref)], axis=0)
        for start in (half, half + height)
    )
    prod = turned(spec[:mine], spec[mine:], filt_re, filt_im)
    cols = [pl.ds(pl.multiple_of(at + core * near_len, near_len), near_len) for at in (0, second_len)]
    back = dot(widened_back(prod), jnp.concatenate([backward_ref[:, col] for col in cols], axis=0))
    unwound = turned(back[:mine], back[mine:], twist_ref[2], -twist_ref[3])
    unwound = jnp.concatenate(unwound, axis=0).astype(jnp.bfloat16)
    total = (dot(inverse_ref[lax.axis_index("col")], unwound) + term_ref[...]).astype(jnp.bfloat16)
    for place in range(parts // 2):
        piece = total[:, place * width : (place + 1) * width].reshape(rows, 2 * half, width)
        out_ref[:, 2 * place], out_ref[:, 2 * place + 1] = crossed(piece[:, :half], piece[:, half:])


def finish_kernel(back_ref, out_ref):
    _, parts, half, _ = back_ref.shape
    cores = []
    for core in range(2):
        shares = [back_ref[:, part].astype(jnp.float32) for part in range(core, parts, 2)]
        cores.append(sum(shares[1:], shares[0]))
    out_ref[:, :half], out_ref[:, half:] = (each.astype(jnp.bfloat16) for each in crossed(*cores))


PARAMS = pltpu.CompilerParams(vmem_limit_bytes=8 * 2**20)
IN_VMEM = pl.BlockSpec(memory_space=pltpu.VMEM)


def call(kernel, outs, *args, flops=None):
    return pl.pallas_call(
        kernel,
        out_shape=[pltpu.VMEM(shape, kind) for shape, kind in outs],
        in_specs=[IN_VMEM] * len(args),
        out_specs=[IN_VMEM] * len(outs),
        compiler_params=PARAMS,
        cost_estimate=flops and pl.CostEstimate(flops=flops, bytes_accessed=0, transcendentals=0),
    )(*(pltpu.with_memory_space_constraint(arg, pltpu.VMEM) for arg in args))


def local_by_channels(signal, filter_real, filter_imag, skip):
    channels, row_count, col_count = signal.shape
    rows = lax.axis_size("row")
    parts = lax.axis_size("col")
    share = channels // rows
    half = row_count // 2
    pairs = [(part, part ^ 1) for part in range(parts)]
    first, block, row, inverse, forward, backward = tables(rows * row_count, parts * col_count, row_count, parts)
    near_len = parts * col_count // 2
    mine = rows * row_count // (parts // 2)
    outs = []

    def exchange(array):
        flat = array.reshape((rows * parts,) + array.shape[2:])
        return lax.all_to_all(flat, ("row", "col"), 0, 0, tiled=True).reshape(array.shape)

    for turn in range(share):
        own = slice(turn * rows, (turn + 1) * rows)
        tall = half + 2 * (row_count // parts)
        args = (signal[own], filter_real[own], filter_imag[own], skip[None])
        send, skips = pl.pallas_call(
            pack_kernel,
            out_shape=[pltpu.VMEM((rows, parts, tall, col_count), jnp.bfloat16), pltpu.VMEM((1, channels), jnp.float32)],
            in_specs=[pl.BlockSpec(memory_space=pltpu.HBM)] * len(args),
            out_specs=[IN_VMEM] * 2,
            scratch_shapes=[
                pltpu.VMEM((rows, row_count, col_count), jnp.bfloat16),
                pltpu.SemaphoreType.DMA((2 * parts + 2,)),
            ],
            compiler_params=PARAMS,
            cost_estimate=pl.CostEstimate(flops=10**9, bytes_accessed=0, transcendentals=0),
        )(*(pltpu.with_memory_space_constraint(arg, pltpu.HBM) for arg in args))
        got = exchange(send)
        swapped = lax.ppermute(got, "col", pairs)
        near = call(
            functools.partial(near_kernel, turn=turn),
            [
                ((2 * mine, 2 * near_len), jnp.float32),
                ((4, mine, near_len), jnp.float32),
                ((rows * row_count, near_len), jnp.float32),
            ],
            *(got, first, block, row, forward, skips),
            flops=10**9,
        )
        (partial_sums,) = call(
            spectrum_kernel,
            [((rows, parts, half, col_count), jnp.bfloat16)],
            *(*near, got, swapped, first, forward, backward, inverse),
        )
        back = exchange(partial_sums)
        outs.append(
            pl.pallas_call(
                finish_kernel,
                out_shape=jax.ShapeDtypeStruct((rows, row_count, col_count), jnp.bfloat16),
                in_specs=[IN_VMEM],
                compiler_params=PARAMS,
            )(pltpu.with_memory_space_constraint(back, pltpu.VMEM))
        )
    return outs[0] if share == 1 else jnp.concatenate(outs, axis=0)


def local(signal, filter_real, filter_imag, skip):
    channels, row_count, col_count = signal.shape
    parts = lax.axis_size("col")
    fits = parts % 2 == 0 and row_count == 8 * parts and col_count % 128 == 0
    if channels % lax.axis_size("row") == 0 and fits:
        return local_by_channels(signal, filter_real, filter_imag, skip)
    return local_by_columns(signal, filter_real, filter_imag, skip)


def solution(mesh):
    in_specs = (P(None, "row", "col"), P(None, "row", "col"), P(None, "row", "col"), P())
    out_specs = P(None, "row", "col")
    return jax.shard_map(local, mesh=mesh, in_specs=in_specs, out_specs=out_specs, check_vma=False)
```

```python
import functools
import math

import jax
import jax.numpy as jnp
import numpy as np
from jax import lax
from jax.experimental import pallas as pl
from jax.experimental.pallas import tpu as pltpu
from jax.sharding import PartitionSpec as P


def phase_table(left_ids, right_ids, modulus):
    product = left_ids[:, None] * right_ids[None, :] % modulus
    angle = -2.0 * math.pi / modulus * product.astype(jnp.float32)
    return (jnp.cos(angle).astype(jnp.bfloat16), jnp.sin(angle).astype(jnp.bfloat16))


def twist_table(left_ids, right_ids, modulus):
    product = left_ids[:, None] * right_ids[None, :] % modulus
    angle = -2.0 * math.pi / modulus * product.astype(jnp.float32)
    return (jnp.cos(angle), jnp.sin(angle))


def column_product(series, phase):
    return jnp.einsum("crn,nk->crk", series, phase, preferred_element_type=jnp.float32)


def row_product(phase, series):
    return jnp.einsum("rn,cnj->crj", phase, series, preferred_element_type=jnp.float32)


def local_by_columns(signal, filter_real, filter_imag, skip):
    channels, row_count, col_count = signal.shape
    first_len = row_count * lax.axis_size("row")
    second_len = col_count * lax.axis_size("col")
    seq_len = first_len * second_len
    row_offset = lax.axis_index("row") * row_count
    col_offset = lax.axis_index("col") * col_count
    own_rows = row_offset + jnp.arange(row_count, dtype=jnp.int32)
    own_cols = col_offset + jnp.arange(col_count, dtype=jnp.int32)
    twist_re, twist_im = twist_table(own_rows, own_cols, seq_len)
    pair_width = col_count // lax.axis_size("row")
    pair_cols = (
        col_offset + lax.axis_index("row") * pair_width + jnp.arange(pair_width, dtype=jnp.int32)
    )
    all_rows = jnp.arange(first_len, dtype=jnp.int32)
    full_re, full_im = phase_table(all_rows, all_rows, first_len)
    columns_whole = lax.all_to_all(signal, "row", split_axis=2, concat_axis=1, tiled=True)
    pair_b_re = row_product(full_re, columns_whole)
    pair_b_im = row_product(full_im, columns_whole)
    pair_tw_re, pair_tw_im = twist_table(all_rows, pair_cols, seq_len)
    pair_mix_re = (pair_b_re * pair_tw_re - pair_b_im * pair_tw_im).astype(jnp.bfloat16)
    pair_mix_im = (pair_b_re * pair_tw_im + pair_b_im * pair_tw_re).astype(jnp.bfloat16)
    mixed_re, mixed_im = (
        lax.all_to_all(pair_mix_re, "row", split_axis=1, concat_axis=2, tiled=True),
        lax.all_to_all(pair_mix_im, "row", split_axis=1, concat_axis=2, tiled=True),
    )
    part_re = lax.all_gather(mixed_re, "col", axis=2, tiled=True)
    part_im = lax.all_gather(mixed_im, "col", axis=2, tiled=True)
    all_cols = jnp.arange(second_len, dtype=jnp.int32)
    phase_re, phase_im = phase_table(all_cols, own_cols, second_len)
    spec_re = column_product(part_re, phase_re) - column_product(part_im, phase_im)
    spec_im = column_product(part_re, phase_im) + column_product(part_im, phase_re)
    prod_re = (spec_re * filter_real - spec_im * filter_imag).astype(jnp.bfloat16)
    prod_im = (spec_re * filter_imag + spec_im * filter_real).astype(jnp.bfloat16)
    part_re = lax.all_gather(prod_re, "col", axis=2, tiled=True)
    part_im = lax.all_gather(prod_im, "col", axis=2, tiled=True)
    new_re = column_product(part_re, phase_re) + column_product(part_im, phase_im)
    new_im = column_product(part_im, phase_re) - column_product(part_re, phase_im)
    unwound_re = (new_re * twist_re + new_im * twist_im).astype(jnp.bfloat16)
    unwound_im = (new_im * twist_re - new_re * twist_im).astype(jnp.bfloat16)
    pair_un_re, pair_un_im = (
        lax.all_to_all(unwound_re, "row", split_axis=2, concat_axis=1, tiled=True),
        lax.all_to_all(unwound_im, "row", split_axis=2, concat_axis=1, tiled=True),
    )
    pair_total = row_product(full_re, pair_un_re) + row_product(full_im, pair_un_im)
    pair_out = (
        pair_total / seq_len + skip[:, None, None] * columns_whole.astype(jnp.float32)
    ).astype(jnp.bfloat16)
    return lax.all_to_all(pair_out, "row", split_axis=1, concat_axis=2, tiled=True)


def row_group(side, member, parts):
    return side + member * (parts - 1 - 2 * side)


def numpy_phase(left_ids, right_ids, modulus):
    product = (left_ids[:, None].astype(np.int64) * right_ids[None, :]) % modulus
    angle = np.float32(-2.0 * math.pi / modulus) * product.astype(np.float32)
    return np.cos(angle), np.sin(angle)


def tables(first_len, second_len, row_count, parts):
    height = row_count // parts
    rows = np.arange(first_len)
    cols = np.arange(second_len)
    by_core = cols.reshape(parts, 2, -1).swapaxes(0, 1).reshape(-1)
    blocks = rows.reshape(-1, row_count)
    groups = [row_group(part // 2, part % 2, parts) for part in range(parts)]
    own = [blocks[:, group * height : (group + 1) * height].reshape(-1) for group in groups]
    first = np.stack(numpy_phase(rows, rows, first_len))
    sides = [[[kind[own[2 * side + core]] for core in range(2)] for kind in first] for side in range(parts // 2)]
    inverse = [
        np.concatenate([kind[:, own[member]] for kind in first for member in (part, part ^ 1)], axis=1)
        for part in range(parts)
    ]
    block_twist = numpy_phase(blocks[:, 0], by_core, first_len * second_len)
    row_twist = numpy_phase(blocks[0], by_core, first_len * second_len)
    forward = np.concatenate(numpy_phase(by_core, cols, second_len), axis=1)
    backward = np.concatenate(numpy_phase(cols, by_core, second_len), axis=1)
    return (
        jnp.asarray(np.array(sides), jnp.bfloat16),
        jnp.asarray(np.stack(block_twist), jnp.float32),
        jnp.asarray(np.stack(row_twist), jnp.float32),
        jnp.asarray(np.stack(inverse), jnp.bfloat16),
        jnp.asarray(forward, jnp.bfloat16),
        jnp.asarray(backward, jnp.bfloat16),
    )


def dot(left, right):
    return jnp.dot(left, right, preferred_element_type=jnp.float32)


def crossed(one, two):
    half = one.shape[-1] // 2
    return (
        jnp.concatenate([one[..., :half], two[..., :half]], axis=-1),
        jnp.concatenate([one[..., half:], two[..., half:]], axis=-1),
    )


def side_and_core():
    part = lax.axis_index("col")
    return part // 2, part % 2


def half_of(core, width):
    return pl.ds(pl.multiple_of(core * width, width), width)


def series_of(ref):
    rows, parts, tall, width = ref.shape
    half = tall // 2
    strips = []
    for part in range(0, parts, 2):
        pair = crossed(ref[:, part, :half, :], ref[:, part + 1, :half, :])
        strips.append(jnp.concatenate(pair, axis=1).reshape(rows * 2 * half, width))
    return jnp.concatenate(strips, axis=1)


def filter_of(ref, start, count):
    rows, parts, _, width = ref.shape
    return jnp.concatenate(
        [ref[:, part, start : start + count, :].astype(jnp.float32).reshape(rows * count, width) for part in range(parts)],
        axis=1,
    )


def twists(block_ref, row_ref, height, side, core, span):
    block_re, block_im = block_ref[0, :, span][:, None, :], block_ref[1, :, span][:, None, :]
    shape = (block_ref.shape[1] * height, span.size)
    re, im = [], []
    for member in (core, 1 - core):
        group = row_group(side, member, row_ref.shape[1] // height)
        at = pl.ds(pl.multiple_of(group * height, height), height)
        row_re, row_im = row_ref[0, at, span][None], row_ref[1, at, span][None]
        re.append((block_re * row_re - block_im * row_im).reshape(shape))
        im.append((block_re * row_im + block_im * row_re).reshape(shape))
    return jnp.concatenate(re, axis=0), jnp.concatenate(im, axis=0)


def turned(re, im, by_re, by_im):
    return re * by_re - im * by_im, re * by_im + im * by_re


def widened(pair):
    re, im = (each.astype(jnp.bfloat16) for each in pair)
    return jnp.concatenate([jnp.concatenate([re, -im], axis=1), jnp.concatenate([im, re], axis=1)], axis=0)


def widened_back(pair):
    re, im = (each.astype(jnp.bfloat16) for each in pair)
    return jnp.concatenate([jnp.concatenate([re, im], axis=1), jnp.concatenate([im, -re], axis=1)], axis=0)


def pack_kernel(signal_ref, real_ref, imag_ref, skip_ref, send_ref, skips_ref, kept_ref, sems):
    _, parts, _, _ = send_ref.shape
    row_count = signal_ref.shape[-2]
    half = row_count // 2
    height = row_count // parts
    copies = [(signal_ref, kept_ref), (skip_ref, skips_ref)]
    for part in range(parts):
        group = row_group(part // 2, part % 2, parts)
        cut = slice(group * height, (group + 1) * height)
        copies.append((real_ref.at[:, cut], send_ref.at[:, part, half : half + height]))
        copies.append((imag_ref.at[:, cut], send_ref.at[:, part, half + height :]))
    copies = [pltpu.make_async_copy(a, b, sems.at[i]) for i, (a, b) in enumerate(copies)]
    for copy in copies:
        copy.start()
    copies[0].wait()
    halves = crossed(kept_ref[:, :half], kept_ref[:, half:])
    for part in range(parts):
        send_ref[:, part, :half] = halves[part % 2]
    for copy in copies[1:]:
        copy.wait()


def half_transform(ref, first_ref, side, core):
    left = [first_ref[side, kind, member] for kind in range(2) for member in (core, 1 - core)]
    both = dot(jnp.concatenate(left, axis=0), series_of(ref))
    mine = both.shape[0] // 2
    return both[:mine], both[mine:]


def forward_rows(forward_ref, core):
    second_len = forward_ref.shape[0]
    rows = half_of(core, second_len // 2)
    return jnp.concatenate([forward_ref[rows, :second_len], forward_ref[rows, second_len:]], axis=0)


def near_kernel(got_ref, first_ref, block_ref, row_ref, forward_ref, spec_ref, twist_ref):
    tall = got_ref.shape[2]
    side, core = side_and_core()
    first_len, second_len = first_ref.shape[-1], forward_ref.shape[0]
    height = tall // 4
    near_len = second_len // 2
    twist = twists(block_ref, row_ref, height, side, core, half_of(core, near_len))
    mixed = turned(*half_transform(got_ref, first_ref, side, core), *twist)
    spec_ref[...] = dot(widened(mixed), forward_rows(forward_ref, core))
    twist_ref[0], twist_ref[1] = twists(block_ref, row_ref, height, side, core, half_of(1 - core, near_len))
    twist_ref[2], twist_ref[3] = (each / (first_len * second_len) for each in twist)


def spectrum_kernel(spec_ref, twist_ref, got_ref, swapped_ref, first_ref, forward_ref, backward_ref, inverse_ref, out_ref):
    rows, parts, tall, width = got_ref.shape
    side, core = side_and_core()
    half, height = tall // 2, tall // 4
    second_len = forward_ref.shape[0]
    near_len = second_len // 2
    mixed = turned(*half_transform(swapped_ref, first_ref, side, core), twist_ref[0], twist_ref[1])
    spec = spec_ref[...] + dot(widened(mixed), forward_rows(forward_ref, 1 - core))
    mine = spec.shape[0] // 2
    filt_re, filt_im = (
        jnp.concatenate([filter_of(ref, start, height) for ref in (got_ref, swapped_ref)], axis=0)
        for start in (half, half + height)
    )
    prod = turned(spec[:mine], spec[mine:], filt_re, filt_im)
    cols = [pl.ds(pl.multiple_of(at + core * near_len, near_len), near_len) for at in (0, second_len)]
    back = dot(widened_back(prod), jnp.concatenate([backward_ref[:, col] for col in cols], axis=0))
    unwound = turned(back[:mine], back[mine:], twist_ref[2], -twist_ref[3])
    unwound = jnp.concatenate(unwound, axis=0).astype(jnp.bfloat16)
    total = dot(inverse_ref[lax.axis_index("col")], unwound).astype(jnp.bfloat16)
    for place in range(parts // 2):
        piece = total[:, place * width : (place + 1) * width].reshape(rows, 2 * half, width)
        out_ref[:, 2 * place], out_ref[:, 2 * place + 1] = crossed(piece[:, :half], piece[:, half:])


def finish_kernel(back_ref, kept_ref, skips_ref, out_ref, *, turn):
    rows, parts, half, _ = back_ref.shape
    cores = []
    for core in range(2):
        shares = [back_ref[:, part].astype(jnp.float32) for part in range(core, parts, 2)]
        cores.append(sum(shares[1:], shares[0]))
    sums = jnp.concatenate(crossed(*cores), axis=1)
    for channel in range(rows):
        at = turn * rows + channel
        term = skips_ref[:, at : at + 1] * kept_ref[channel].astype(jnp.float32)
        out_ref[channel] = (sums[channel] + term).astype(jnp.bfloat16)


PARAMS = pltpu.CompilerParams(vmem_limit_bytes=8 * 2**20)
IN_VMEM = pl.BlockSpec(memory_space=pltpu.VMEM)


def call(kernel, outs, *args, flops=None):
    return pl.pallas_call(
        kernel,
        out_shape=[pltpu.VMEM(shape, kind) for shape, kind in outs],
        in_specs=[IN_VMEM] * len(args),
        out_specs=[IN_VMEM] * len(outs),
        compiler_params=PARAMS,
        cost_estimate=flops and pl.CostEstimate(flops=flops, bytes_accessed=0, transcendentals=0),
    )(*(pltpu.with_memory_space_constraint(arg, pltpu.VMEM) for arg in args))


def local_by_channels(signal, filter_real, filter_imag, skip):
    channels, row_count, col_count = signal.shape
    rows = lax.axis_size("row")
    parts = lax.axis_size("col")
    share = channels // rows
    half = row_count // 2
    pairs = [(part, part ^ 1) for part in range(parts)]
    first, block, row, inverse, forward, backward = tables(rows * row_count, parts * col_count, row_count, parts)
    near_len = parts * col_count // 2
    mine = rows * row_count // (parts // 2)
    outs = []

    def exchange(array):
        flat = array.reshape((rows * parts,) + array.shape[2:])
        return lax.all_to_all(flat, ("row", "col"), 0, 0, tiled=True).reshape(array.shape)

    for turn in range(share):
        own = slice(turn * rows, (turn + 1) * rows)
        tall = half + 2 * (row_count // parts)
        args = (signal[own], filter_real[own], filter_imag[own], skip[None])
        send, skips, kept = pl.pallas_call(
            pack_kernel,
            out_shape=[
                pltpu.VMEM((rows, parts, tall, col_count), jnp.bfloat16),
                pltpu.VMEM((1, channels), jnp.float32),
                pltpu.VMEM((rows, row_count, col_count), jnp.bfloat16),
            ],
            in_specs=[pl.BlockSpec(memory_space=pltpu.HBM)] * len(args),
            out_specs=[IN_VMEM] * 3,
            scratch_shapes=[pltpu.SemaphoreType.DMA((2 * parts + 2,))],
            compiler_params=PARAMS,
            cost_estimate=pl.CostEstimate(flops=10**9, bytes_accessed=0, transcendentals=0),
        )(*(pltpu.with_memory_space_constraint(arg, pltpu.HBM) for arg in args))
        got = exchange(send)
        swapped = lax.ppermute(got, "col", pairs)
        near = call(
            near_kernel,
            [((2 * mine, 2 * near_len), jnp.float32), ((4, mine, near_len), jnp.float32)],
            *(got, first, block, row, forward),
            flops=10**9,
        )
        (partial_sums,) = call(
            spectrum_kernel,
            [((rows, parts, half, col_count), jnp.bfloat16)],
            *(*near, got, swapped, first, forward, backward, inverse),
        )
        back = exchange(partial_sums)
        outs.append(
            pl.pallas_call(
                functools.partial(finish_kernel, turn=turn),
                out_shape=jax.ShapeDtypeStruct((rows, row_count, col_count), jnp.bfloat16),
                in_specs=[IN_VMEM] * 3,
                compiler_params=PARAMS,
            )(*(pltpu.with_memory_space_constraint(arg, pltpu.VMEM) for arg in (back, kept, skips)))
        )
    return outs[0] if share == 1 else jnp.concatenate(outs, axis=0)


def local(signal, filter_real, filter_imag, skip):
    channels, row_count, col_count = signal.shape
    parts = lax.axis_size("col")
    fits = parts % 2 == 0 and row_count == 8 * parts and col_count % 128 == 0
    if channels % lax.axis_size("row") == 0 and fits:
        return local_by_channels(signal, filter_real, filter_imag, skip)
    return local_by_columns(signal, filter_real, filter_imag, skip)


def solution(mesh):
    in_specs = (P(None, "row", "col"), P(None, "row", "col"), P(None, "row", "col"), P())
    out_specs = P(None, "row", "col")
    return jax.shard_map(local, mesh=mesh, in_specs=in_specs, out_specs=out_specs, check_vma=False)
```

```python
import functools
import math

import jax
import jax.numpy as jnp
import numpy as np
from jax import lax
from jax.experimental import pallas as pl
from jax.experimental.pallas import tpu as pltpu
from jax.sharding import PartitionSpec as P


def phase_table(left_ids, right_ids, modulus):
    product = left_ids[:, None] * right_ids[None, :] % modulus
    angle = -2.0 * math.pi / modulus * product.astype(jnp.float32)
    return (jnp.cos(angle).astype(jnp.bfloat16), jnp.sin(angle).astype(jnp.bfloat16))


def twist_table(left_ids, right_ids, modulus):
    product = left_ids[:, None] * right_ids[None, :] % modulus
    angle = -2.0 * math.pi / modulus * product.astype(jnp.float32)
    return (jnp.cos(angle), jnp.sin(angle))


def column_product(series, phase):
    return jnp.einsum("crn,nk->crk", series, phase, preferred_element_type=jnp.float32)


def row_product(phase, series):
    return jnp.einsum("rn,cnj->crj", phase, series, preferred_element_type=jnp.float32)


def local_by_columns(signal, filter_real, filter_imag, skip):
    channels, row_count, col_count = signal.shape
    first_len = row_count * lax.axis_size("row")
    second_len = col_count * lax.axis_size("col")
    seq_len = first_len * second_len
    row_offset = lax.axis_index("row") * row_count
    col_offset = lax.axis_index("col") * col_count
    own_rows = row_offset + jnp.arange(row_count, dtype=jnp.int32)
    own_cols = col_offset + jnp.arange(col_count, dtype=jnp.int32)
    twist_re, twist_im = twist_table(own_rows, own_cols, seq_len)
    pair_width = col_count // lax.axis_size("row")
    pair_cols = (
        col_offset + lax.axis_index("row") * pair_width + jnp.arange(pair_width, dtype=jnp.int32)
    )
    all_rows = jnp.arange(first_len, dtype=jnp.int32)
    full_re, full_im = phase_table(all_rows, all_rows, first_len)
    columns_whole = lax.all_to_all(signal, "row", split_axis=2, concat_axis=1, tiled=True)
    pair_b_re = row_product(full_re, columns_whole)
    pair_b_im = row_product(full_im, columns_whole)
    pair_tw_re, pair_tw_im = twist_table(all_rows, pair_cols, seq_len)
    pair_mix_re = (pair_b_re * pair_tw_re - pair_b_im * pair_tw_im).astype(jnp.bfloat16)
    pair_mix_im = (pair_b_re * pair_tw_im + pair_b_im * pair_tw_re).astype(jnp.bfloat16)
    mixed_re, mixed_im = (
        lax.all_to_all(pair_mix_re, "row", split_axis=1, concat_axis=2, tiled=True),
        lax.all_to_all(pair_mix_im, "row", split_axis=1, concat_axis=2, tiled=True),
    )
    part_re = lax.all_gather(mixed_re, "col", axis=2, tiled=True)
    part_im = lax.all_gather(mixed_im, "col", axis=2, tiled=True)
    all_cols = jnp.arange(second_len, dtype=jnp.int32)
    phase_re, phase_im = phase_table(all_cols, own_cols, second_len)
    spec_re = column_product(part_re, phase_re) - column_product(part_im, phase_im)
    spec_im = column_product(part_re, phase_im) + column_product(part_im, phase_re)
    prod_re = (spec_re * filter_real - spec_im * filter_imag).astype(jnp.bfloat16)
    prod_im = (spec_re * filter_imag + spec_im * filter_real).astype(jnp.bfloat16)
    part_re = lax.all_gather(prod_re, "col", axis=2, tiled=True)
    part_im = lax.all_gather(prod_im, "col", axis=2, tiled=True)
    new_re = column_product(part_re, phase_re) + column_product(part_im, phase_im)
    new_im = column_product(part_im, phase_re) - column_product(part_re, phase_im)
    unwound_re = (new_re * twist_re + new_im * twist_im).astype(jnp.bfloat16)
    unwound_im = (new_im * twist_re - new_re * twist_im).astype(jnp.bfloat16)
    pair_un_re, pair_un_im = (
        lax.all_to_all(unwound_re, "row", split_axis=2, concat_axis=1, tiled=True),
        lax.all_to_all(unwound_im, "row", split_axis=2, concat_axis=1, tiled=True),
    )
    pair_total = row_product(full_re, pair_un_re) + row_product(full_im, pair_un_im)
    pair_out = (
        pair_total / seq_len + skip[:, None, None] * columns_whole.astype(jnp.float32)
    ).astype(jnp.bfloat16)
    return lax.all_to_all(pair_out, "row", split_axis=1, concat_axis=2, tiled=True)


def row_group(side, member, parts):
    return side + member * (parts - 1 - 2 * side)


def numpy_phase(left_ids, right_ids, modulus):
    product = (left_ids[:, None].astype(np.int64) * right_ids[None, :]) % modulus
    angle = np.float32(-2.0 * math.pi / modulus) * product.astype(np.float32)
    return np.cos(angle), np.sin(angle)


def tables(first_len, second_len, row_count, parts):
    height = row_count // parts
    rows = np.arange(first_len)
    cols = np.arange(second_len)
    by_core = cols.reshape(parts, 2, -1).swapaxes(0, 1).reshape(-1)
    blocks = rows.reshape(-1, row_count)
    groups = [row_group(part // 2, part % 2, parts) for part in range(parts)]
    own = [blocks[:, group * height : (group + 1) * height].reshape(-1) for group in groups]
    first = np.stack(numpy_phase(rows, rows, first_len))
    sides = [[[kind[own[2 * side + core]] for core in range(2)] for kind in first] for side in range(parts // 2)]
    inverse = [
        np.concatenate([kind[:, own[member]] for kind in first for member in (part, part ^ 1)], axis=1)
        for part in range(parts)
    ]
    block_twist = numpy_phase(blocks[:, 0], by_core, first_len * second_len)
    row_twist = numpy_phase(blocks[0], by_core, first_len * second_len)
    forward = np.concatenate(numpy_phase(by_core, cols, second_len), axis=1)
    backward = np.concatenate(numpy_phase(cols, by_core, second_len), axis=1)
    return (
        jnp.asarray(np.array(sides), jnp.bfloat16),
        jnp.asarray(np.stack(block_twist), jnp.float32),
        jnp.asarray(np.stack(row_twist), jnp.float32),
        jnp.asarray(np.stack(inverse), jnp.bfloat16),
        jnp.asarray(forward, jnp.bfloat16),
        jnp.asarray(backward, jnp.bfloat16),
    )


def dot(left, right):
    return jnp.dot(left, right, preferred_element_type=jnp.float32)


def crossed(one, two):
    half = one.shape[-1] // 2
    return (
        jnp.concatenate([one[..., :half], two[..., :half]], axis=-1),
        jnp.concatenate([one[..., half:], two[..., half:]], axis=-1),
    )


def in_left(array):
    axis = array.ndim - 1
    return lax.broadcasted_iota(jnp.int32, array.shape, axis) < array.shape[axis] // 2


def turned_over(array):
    half = array.shape[-1] // 2
    return jnp.concatenate([array[..., half:], array[..., :half]], axis=-1)


def side_and_core():
    part = lax.axis_index("col")
    return part // 2, part % 2


def half_of(core, width):
    return pl.ds(pl.multiple_of(core * width, width), width)


def series_of(ref):
    rows, parts, tall, width = ref.shape
    half = tall // 2
    strips = []
    for part in range(0, parts, 2):
        even, odd = ref[:, part, :half, :], ref[:, part + 1, :half, :]
        left = in_left(even)
        pair = [jnp.where(left, even, odd), turned_over(jnp.where(left, odd, even))]
        strips.append(jnp.concatenate(pair, axis=1).reshape(rows * 2 * half, width))
    return jnp.concatenate(strips, axis=1)


def filter_of(ref, start, count):
    rows, parts, _, width = ref.shape
    return jnp.concatenate(
        [ref[:, part, start : start + count, :].astype(jnp.float32).reshape(rows * count, width) for part in range(parts)],
        axis=1,
    )


def twists(block_ref, row_ref, height, side, core, span):
    block_re, block_im = block_ref[0, :, span][:, None, :], block_ref[1, :, span][:, None, :]
    shape = (block_ref.shape[1] * height, span.size)
    re, im = [], []
    for member in (core, 1 - core):
        group = row_group(side, member, row_ref.shape[1] // height)
        at = pl.ds(pl.multiple_of(group * height, height), height)
        row_re, row_im = row_ref[0, at, span][None], row_ref[1, at, span][None]
        re.append((block_re * row_re - block_im * row_im).reshape(shape))
        im.append((block_re * row_im + block_im * row_re).reshape(shape))
    return jnp.concatenate(re, axis=0), jnp.concatenate(im, axis=0)


def turned(re, im, by_re, by_im):
    return re * by_re - im * by_im, re * by_im + im * by_re


def widened(pair):
    re, im = (each.astype(jnp.bfloat16) for each in pair)
    return jnp.concatenate([jnp.concatenate([re, -im], axis=1), jnp.concatenate([im, re], axis=1)], axis=0)


def widened_back(pair):
    re, im = (each.astype(jnp.bfloat16) for each in pair)
    return jnp.concatenate([jnp.concatenate([re, im], axis=1), jnp.concatenate([im, -re], axis=1)], axis=0)


def pack_kernel(signal_ref, real_ref, imag_ref, skip_ref, send_ref, skips_ref, kept_ref, sems):
    _, parts, _, _ = send_ref.shape
    row_count = signal_ref.shape[-2]
    half = row_count // 2
    height = row_count // parts
    copies = [(signal_ref, kept_ref), (skip_ref, skips_ref)]
    for part in range(parts):
        group = row_group(part // 2, part % 2, parts)
        cut = slice(group * height, (group + 1) * height)
        copies.append((real_ref.at[:, cut], send_ref.at[:, part, half : half + height]))
        copies.append((imag_ref.at[:, cut], send_ref.at[:, part, half + height :]))
    copies = [pltpu.make_async_copy(a, b, sems.at[i]) for i, (a, b) in enumerate(copies)]
    for copy in copies:
        copy.start()
    copies[0].wait()
    is_even = side_and_core()[1] == 0
    upper, lower = kept_ref[:, :half], kept_ref[:, half:]
    halves = crossed(jnp.where(is_even, upper, lower), jnp.where(is_even, lower, upper))
    for part in range(parts):
        send_ref[:, part, :half] = halves[part % 2]
    for copy in copies[1:]:
        copy.wait()


def half_transform(ref, first_ref, side, core):
    left = [first_ref[side, kind, member] for kind in range(2) for member in (core, 1 - core)]
    both = dot(jnp.concatenate(left, axis=0), series_of(ref))
    mine = both.shape[0] // 2
    return both[:mine], both[mine:]


def forward_rows(forward_ref, core):
    second_len = forward_ref.shape[0]
    rows = half_of(core, second_len // 2)
    return jnp.concatenate([forward_ref[rows, :second_len], forward_ref[rows, second_len:]], axis=0)


def near_kernel(got_ref, first_ref, block_ref, row_ref, forward_ref, spec_ref, twist_ref):
    tall = got_ref.shape[2]
    side, core = side_and_core()
    first_len, second_len = first_ref.shape[-1], forward_ref.shape[0]
    height = tall // 4
    near_len = second_len // 2
    twist = twists(block_ref, row_ref, height, side, core, half_of(core, near_len))
    mixed = turned(*half_transform(got_ref, first_ref, side, core), *twist)
    spec_ref[...] = dot(widened(mixed), forward_rows(forward_ref, core))
    twist_ref[0], twist_ref[1] = twists(block_ref, row_ref, height, side, core, half_of(1 - core, near_len))
    twist_ref[2], twist_ref[3] = (each / (first_len * second_len) for each in twist)


def spectrum_kernel(spec_ref, twist_ref, got_ref, swapped_ref, first_ref, forward_ref, backward_ref, inverse_ref, out_ref):
    rows, parts, tall, width = got_ref.shape
    side, core = side_and_core()
    half, height = tall // 2, tall // 4
    second_len = forward_ref.shape[0]
    near_len = second_len // 2
    mixed = turned(*half_transform(swapped_ref, first_ref, side, core), twist_ref[0], twist_ref[1])
    spec = spec_ref[...] + dot(widened(mixed), forward_rows(forward_ref, 1 - core))
    mine = spec.shape[0] // 2
    filt_re, filt_im = (
        jnp.concatenate([filter_of(ref, start, height) for ref in (got_ref, swapped_ref)], axis=0)
        for start in (half, half + height)
    )
    prod = turned(spec[:mine], spec[mine:], filt_re, filt_im)
    cols = [pl.ds(pl.multiple_of(at + core * near_len, near_len), near_len) for at in (0, second_len)]
    back = dot(widened_back(prod), jnp.concatenate([backward_ref[:, col] for col in cols], axis=0))
    unwound = turned(back[:mine], back[mine:], twist_ref[2], -twist_ref[3])
    unwound = jnp.concatenate(unwound, axis=0).astype(jnp.bfloat16)
    total = dot(inverse_ref[lax.axis_index("col")], unwound).astype(jnp.bfloat16)
    for place in range(parts // 2):
        piece = total[:, place * width : (place + 1) * width].reshape(rows, 2 * half, width)
        upper, lower = piece[:, :half], turned_over(piece[:, half:])
        left = in_left(upper)
        out_ref[:, 2 * place] = jnp.where(left, upper, lower)
        out_ref[:, 2 * place + 1] = jnp.where(left, lower, upper)


def finish_kernel(back_ref, kept_ref, skips_ref, out_ref, *, turn):
    rows, parts, half, _ = back_ref.shape
    cores = []
    for core in range(2):
        shares = [back_ref[:, part].astype(jnp.float32) for part in range(core, parts, 2)]
        cores.append(sum(shares[1:], shares[0]))
    one, two = crossed(*cores)
    is_even = side_and_core()[1] == 0
    sums = jnp.concatenate([jnp.where(is_even, one, two), jnp.where(is_even, two, one)], axis=1)
    for channel in range(rows):
        at = turn * rows + channel
        term = skips_ref[:, at : at + 1] * kept_ref[channel].astype(jnp.float32)
        out_ref[channel] = (sums[channel] + term).astype(jnp.bfloat16)


PARAMS = pltpu.CompilerParams(vmem_limit_bytes=8 * 2**20)
IN_VMEM = pl.BlockSpec(memory_space=pltpu.VMEM)


def call(kernel, outs, *args, flops=None):
    return pl.pallas_call(
        kernel,
        out_shape=[pltpu.VMEM(shape, kind) for shape, kind in outs],
        in_specs=[IN_VMEM] * len(args),
        out_specs=[IN_VMEM] * len(outs),
        compiler_params=PARAMS,
        cost_estimate=flops and pl.CostEstimate(flops=flops, bytes_accessed=0, transcendentals=0),
    )(*(pltpu.with_memory_space_constraint(arg, pltpu.VMEM) for arg in args))


def local_by_channels(signal, filter_real, filter_imag, skip):
    channels, row_count, col_count = signal.shape
    rows = lax.axis_size("row")
    parts = lax.axis_size("col")
    share = channels // rows
    half = row_count // 2
    pairs = [(part, part ^ 1) for part in range(parts)]
    first, block, row, inverse, forward, backward = tables(rows * row_count, parts * col_count, row_count, parts)
    near_len = parts * col_count // 2
    mine = rows * row_count // (parts // 2)
    outs = []

    def exchange(array):
        flat = array.reshape((rows * parts,) + array.shape[2:])
        return lax.all_to_all(flat, ("row", "col"), 0, 0, tiled=True).reshape(array.shape)

    for turn in range(share):
        own = slice(turn * rows, (turn + 1) * rows)
        tall = half + 2 * (row_count // parts)
        args = (signal[own], filter_real[own], filter_imag[own], skip[None])
        send, skips, kept = pl.pallas_call(
            pack_kernel,
            out_shape=[
                pltpu.VMEM((rows, parts, tall, col_count), jnp.bfloat16),
                pltpu.VMEM((1, channels), jnp.float32),
                pltpu.VMEM((rows, row_count, col_count), jnp.bfloat16),
            ],
            in_specs=[pl.BlockSpec(memory_space=pltpu.HBM)] * len(args),
            out_specs=[IN_VMEM] * 3,
            scratch_shapes=[pltpu.SemaphoreType.DMA((2 * parts + 2,))],
            compiler_params=PARAMS,
            cost_estimate=pl.CostEstimate(flops=10**9, bytes_accessed=0, transcendentals=0),
        )(*(pltpu.with_memory_space_constraint(arg, pltpu.HBM) for arg in args))
        got = exchange(send)
        swapped = lax.ppermute(got, "col", pairs)
        near = call(
            near_kernel,
            [((2 * mine, 2 * near_len), jnp.float32), ((4, mine, near_len), jnp.float32)],
            *(got, first, block, row, forward),
            flops=10**9,
        )
        (partial_sums,) = call(
            spectrum_kernel,
            [((rows, parts, half, col_count), jnp.bfloat16)],
            *(*near, got, swapped, first, forward, backward, inverse),
        )
        back = exchange(partial_sums)
        outs.append(
            pl.pallas_call(
                functools.partial(finish_kernel, turn=turn),
                out_shape=jax.ShapeDtypeStruct((rows, row_count, col_count), jnp.bfloat16),
                in_specs=[IN_VMEM] * 3,
                compiler_params=PARAMS,
            )(*(pltpu.with_memory_space_constraint(arg, pltpu.VMEM) for arg in (back, kept, skips)))
        )
    return outs[0] if share == 1 else jnp.concatenate(outs, axis=0)


def local(signal, filter_real, filter_imag, skip):
    channels, row_count, col_count = signal.shape
    parts = lax.axis_size("col")
    fits = parts % 2 == 0 and row_count == 8 * parts and col_count % 128 == 0
    if channels % lax.axis_size("row") == 0 and fits:
        return local_by_channels(signal, filter_real, filter_imag, skip)
    return local_by_columns(signal, filter_real, filter_imag, skip)


def solution(mesh):
    in_specs = (P(None, "row", "col"), P(None, "row", "col"), P(None, "row", "col"), P())
    out_specs = P(None, "row", "col")
    return jax.shard_map(local, mesh=mesh, in_specs=in_specs, out_specs=out_specs, check_vma=False)
```

```python
import functools
import math

import jax
import jax.numpy as jnp
import numpy as np
from jax import lax
from jax.experimental import pallas as pl
from jax.experimental.pallas import tpu as pltpu
from jax.sharding import PartitionSpec as P


def phase_table(left_ids, right_ids, modulus):
    product = left_ids[:, None] * right_ids[None, :] % modulus
    angle = -2.0 * math.pi / modulus * product.astype(jnp.float32)
    return (jnp.cos(angle).astype(jnp.bfloat16), jnp.sin(angle).astype(jnp.bfloat16))


def twist_table(left_ids, right_ids, modulus):
    product = left_ids[:, None] * right_ids[None, :] % modulus
    angle = -2.0 * math.pi / modulus * product.astype(jnp.float32)
    return (jnp.cos(angle), jnp.sin(angle))


def column_product(series, phase):
    return jnp.einsum("crn,nk->crk", series, phase, preferred_element_type=jnp.float32)


def row_product(phase, series):
    return jnp.einsum("rn,cnj->crj", phase, series, preferred_element_type=jnp.float32)


def local_by_columns(signal, filter_real, filter_imag, skip):
    channels, row_count, col_count = signal.shape
    first_len = row_count * lax.axis_size("row")
    second_len = col_count * lax.axis_size("col")
    seq_len = first_len * second_len
    row_offset = lax.axis_index("row") * row_count
    col_offset = lax.axis_index("col") * col_count
    own_rows = row_offset + jnp.arange(row_count, dtype=jnp.int32)
    own_cols = col_offset + jnp.arange(col_count, dtype=jnp.int32)
    twist_re, twist_im = twist_table(own_rows, own_cols, seq_len)
    pair_width = col_count // lax.axis_size("row")
    pair_cols = (
        col_offset + lax.axis_index("row") * pair_width + jnp.arange(pair_width, dtype=jnp.int32)
    )
    all_rows = jnp.arange(first_len, dtype=jnp.int32)
    full_re, full_im = phase_table(all_rows, all_rows, first_len)
    columns_whole = lax.all_to_all(signal, "row", split_axis=2, concat_axis=1, tiled=True)
    pair_b_re = row_product(full_re, columns_whole)
    pair_b_im = row_product(full_im, columns_whole)
    pair_tw_re, pair_tw_im = twist_table(all_rows, pair_cols, seq_len)
    pair_mix_re = (pair_b_re * pair_tw_re - pair_b_im * pair_tw_im).astype(jnp.bfloat16)
    pair_mix_im = (pair_b_re * pair_tw_im + pair_b_im * pair_tw_re).astype(jnp.bfloat16)
    mixed_re, mixed_im = (
        lax.all_to_all(pair_mix_re, "row", split_axis=1, concat_axis=2, tiled=True),
        lax.all_to_all(pair_mix_im, "row", split_axis=1, concat_axis=2, tiled=True),
    )
    part_re = lax.all_gather(mixed_re, "col", axis=2, tiled=True)
    part_im = lax.all_gather(mixed_im, "col", axis=2, tiled=True)
    all_cols = jnp.arange(second_len, dtype=jnp.int32)
    phase_re, phase_im = phase_table(all_cols, own_cols, second_len)
    spec_re = column_product(part_re, phase_re) - column_product(part_im, phase_im)
    spec_im = column_product(part_re, phase_im) + column_product(part_im, phase_re)
    prod_re = (spec_re * filter_real - spec_im * filter_imag).astype(jnp.bfloat16)
    prod_im = (spec_re * filter_imag + spec_im * filter_real).astype(jnp.bfloat16)
    part_re = lax.all_gather(prod_re, "col", axis=2, tiled=True)
    part_im = lax.all_gather(prod_im, "col", axis=2, tiled=True)
    new_re = column_product(part_re, phase_re) + column_product(part_im, phase_im)
    new_im = column_product(part_im, phase_re) - column_product(part_re, phase_im)
    unwound_re = (new_re * twist_re + new_im * twist_im).astype(jnp.bfloat16)
    unwound_im = (new_im * twist_re - new_re * twist_im).astype(jnp.bfloat16)
    pair_un_re, pair_un_im = (
        lax.all_to_all(unwound_re, "row", split_axis=2, concat_axis=1, tiled=True),
        lax.all_to_all(unwound_im, "row", split_axis=2, concat_axis=1, tiled=True),
    )
    pair_total = row_product(full_re, pair_un_re) + row_product(full_im, pair_un_im)
    pair_out = (
        pair_total / seq_len + skip[:, None, None] * columns_whole.astype(jnp.float32)
    ).astype(jnp.bfloat16)
    return lax.all_to_all(pair_out, "row", split_axis=1, concat_axis=2, tiled=True)


def row_group(side, member, parts):
    return side + member * (parts - 1 - 2 * side)


def numpy_phase(left_ids, right_ids, modulus):
    product = (left_ids[:, None].astype(np.int64) * right_ids[None, :]) % modulus
    angle = np.float32(-2.0 * math.pi / modulus) * product.astype(np.float32)
    return np.cos(angle), np.sin(angle)


def tables(first_len, second_len, row_count, parts):
    height = row_count // parts
    rows = np.arange(first_len)
    cols = np.arange(second_len)
    by_core = cols.reshape(parts, 2, -1).swapaxes(0, 1).reshape(-1)
    blocks = rows.reshape(-1, row_count)
    groups = [row_group(part // 2, part % 2, parts) for part in range(parts)]
    own = [blocks[:, group * height : (group + 1) * height].reshape(-1) for group in groups]
    first = np.stack(numpy_phase(rows, rows, first_len))
    sides = [[[kind[own[2 * side + core]] for core in range(2)] for kind in first] for side in range(parts // 2)]
    inverse = [
        np.concatenate([kind[:, own[member]] for kind in first for member in (part, part ^ 1)], axis=1)
        for part in range(parts)
    ]
    block_twist = numpy_phase(blocks[:, 0], by_core, first_len * second_len)
    row_twist = numpy_phase(blocks[0], by_core, first_len * second_len)
    forward = np.concatenate(numpy_phase(by_core, cols, second_len), axis=1)
    backward = np.concatenate(numpy_phase(cols, by_core, second_len), axis=1)
    return (
        jnp.asarray(np.array(sides), jnp.bfloat16),
        jnp.asarray(np.stack(block_twist), jnp.float32),
        jnp.asarray(np.stack(row_twist), jnp.float32),
        jnp.asarray(np.stack(inverse), jnp.bfloat16),
        jnp.asarray(forward, jnp.bfloat16),
        jnp.asarray(backward, jnp.bfloat16),
    )


def dot(left, right):
    return jnp.dot(left, right, preferred_element_type=jnp.float32)


def crossed(one, two):
    half = one.shape[-1] // 2
    return (
        jnp.concatenate([one[..., :half], two[..., :half]], axis=-1),
        jnp.concatenate([one[..., half:], two[..., half:]], axis=-1),
    )


def side_and_core():
    part = lax.axis_index("col")
    return part // 2, part % 2


def half_of(core, width):
    return pl.ds(pl.multiple_of(core * width, width), width)


def series_of(ref):
    rows, parts, tall, width = ref.shape
    half = tall // 2
    strips = []
    for part in range(0, parts, 2):
        pair = crossed(ref[:, part, :half, :], ref[:, part + 1, :half, :])
        strips.append(jnp.concatenate(pair, axis=1).reshape(rows * 2 * half, width))
    return jnp.concatenate(strips, axis=1)


def filter_of(ref, start, count):
    rows, parts, _, width = ref.shape
    return jnp.concatenate(
        [ref[:, part, start : start + count, :].astype(jnp.float32).reshape(rows * count, width) for part in range(parts)],
        axis=1,
    )


def twists(block_ref, row_ref, height, side, core, span):
    block_re, block_im = block_ref[0, :, span][:, None, :], block_ref[1, :, span][:, None, :]
    shape = (block_ref.shape[1] * height, span.size)
    re, im = [], []
    for member in (core, 1 - core):
        group = row_group(side, member, row_ref.shape[1] // height)
        at = pl.ds(pl.multiple_of(group * height, height), height)
        row_re, row_im = row_ref[0, at, span][None], row_ref[1, at, span][None]
        re.append((block_re * row_re - block_im * row_im).reshape(shape))
        im.append((block_re * row_im + block_im * row_re).reshape(shape))
    return jnp.concatenate(re, axis=0), jnp.concatenate(im, axis=0)


def turned(re, im, by_re, by_im):
    return re * by_re - im * by_im, re * by_im + im * by_re


def widened(pair):
    re, im = (each.astype(jnp.bfloat16) for each in pair)
    return jnp.concatenate([jnp.concatenate([re, -im], axis=1), jnp.concatenate([im, re], axis=1)], axis=0)


def pack_kernel(signal_ref, real_ref, imag_ref, skip_ref, send_ref, skips_ref, kept_ref, sems):
    _, parts, _, _ = send_ref.shape
    row_count = signal_ref.shape[-2]
    half = row_count // 2
    height = row_count // parts
    copies = [(signal_ref, kept_ref), (skip_ref, skips_ref)]
    for part in range(parts):
        group = row_group(part // 2, part % 2, parts)
        cut = slice(group * height, (group + 1) * height)
        copies.append((real_ref.at[:, cut], send_ref.at[:, part, half : half + height]))
        copies.append((imag_ref.at[:, cut], send_ref.at[:, part, half + height :]))
    copies = [pltpu.make_async_copy(a, b, sems.at[i]) for i, (a, b) in enumerate(copies)]
    for copy in copies:
        copy.start()
    copies[0].wait()
    halves = crossed(kept_ref[:, :half], kept_ref[:, half:])
    for part in range(parts):
        send_ref[:, part, :half] = halves[part % 2]
    for copy in copies[1:]:
        copy.wait()


def half_transform(ref, first_ref, side, core):
    left = [first_ref[side, kind, member] for kind in range(2) for member in (core, 1 - core)]
    both = dot(jnp.concatenate(left, axis=0), series_of(ref))
    mine = both.shape[0] // 2
    return both[:mine], both[mine:]


def forward_rows(forward_ref, core):
    second_len = forward_ref.shape[0]
    rows = half_of(core, second_len // 2)
    return jnp.concatenate([forward_ref[rows, :second_len], forward_ref[rows, second_len:]], axis=0)


def near_kernel(got_ref, first_ref, block_ref, row_ref, forward_ref, spec_ref, twist_ref):
    tall = got_ref.shape[2]
    side, core = side_and_core()
    first_len, second_len = first_ref.shape[-1], forward_ref.shape[0]
    height = tall // 4
    near_len = second_len // 2
    twist = twists(block_ref, row_ref, height, side, core, half_of(core, near_len))
    mixed = turned(*half_transform(got_ref, first_ref, side, core), *twist)
    spec_ref[...] = dot(widened(mixed), forward_rows(forward_ref, core))
    twist_ref[0], twist_ref[1] = twists(block_ref, row_ref, height, side, core, half_of(1 - core, near_len))
    twist_ref[2], twist_ref[3] = (each / (first_len * second_len) for each in twist)


def spectrum_kernel(spec_ref, twist_ref, got_ref, swapped_ref, first_ref, forward_ref, backward_ref, inverse_ref, out_ref):
    rows, parts, tall, width = got_ref.shape
    side, core = side_and_core()
    half, height = tall // 2, tall // 4
    second_len = forward_ref.shape[0]
    near_len = second_len // 2
    mixed = turned(*half_transform(swapped_ref, first_ref, side, core), twist_ref[0], twist_ref[1])
    spec = spec_ref[...] + dot(widened(mixed), forward_rows(forward_ref, 1 - core))
    mine = spec.shape[0] // 2
    filt_re, filt_im = (
        jnp.concatenate([filter_of(ref, start, height) for ref in (got_ref, swapped_ref)], axis=0)
        for start in (half, half + height)
    )
    prod = turned(spec[:mine], spec[mine:], filt_re, filt_im)
    cols = [pl.ds(pl.multiple_of(at + core * near_len, near_len), near_len) for at in (0, second_len)]
    prod = jnp.concatenate(prod, axis=0).astype(jnp.bfloat16)
    both = dot(prod, jnp.concatenate([backward_ref[:, col] for col in cols], axis=1))
    back_re = both[:mine, :near_len] + both[mine:, near_len:]
    back_im = both[mine:, :near_len] - both[:mine, near_len:]
    unwound = turned(back_re, back_im, twist_ref[2], -twist_ref[3])
    unwound = jnp.concatenate(unwound, axis=0).astype(jnp.bfloat16)
    total = dot(inverse_ref[lax.axis_index("col")], unwound).astype(jnp.bfloat16)
    for place in range(parts // 2):
        piece = total[:, place * width : (place + 1) * width].reshape(rows, 2 * half, width)
        out_ref[:, 2 * place], out_ref[:, 2 * place + 1] = crossed(piece[:, :half], piece[:, half:])


def finish_kernel(back_ref, kept_ref, skips_ref, out_ref, *, turn):
    rows, parts, half, _ = back_ref.shape
    cores = []
    for core in range(2):
        shares = [back_ref[:, part].astype(jnp.float32) for part in range(core, parts, 2)]
        cores.append(sum(shares[1:], shares[0]))
    sums = jnp.concatenate(crossed(*cores), axis=1)
    for channel in range(rows):
        at = turn * rows + channel
        term = skips_ref[:, at : at + 1] * kept_ref[channel].astype(jnp.float32)
        out_ref[channel] = (sums[channel] + term).astype(jnp.bfloat16)


PARAMS = pltpu.CompilerParams(vmem_limit_bytes=8 * 2**20)
IN_VMEM = pl.BlockSpec(memory_space=pltpu.VMEM)


def call(kernel, outs, *args, flops=None):
    return pl.pallas_call(
        kernel,
        out_shape=[pltpu.VMEM(shape, kind) for shape, kind in outs],
        in_specs=[IN_VMEM] * len(args),
        out_specs=[IN_VMEM] * len(outs),
        compiler_params=PARAMS,
        cost_estimate=flops and pl.CostEstimate(flops=flops, bytes_accessed=0, transcendentals=0),
    )(*(pltpu.with_memory_space_constraint(arg, pltpu.VMEM) for arg in args))


def local_by_channels(signal, filter_real, filter_imag, skip):
    channels, row_count, col_count = signal.shape
    rows = lax.axis_size("row")
    parts = lax.axis_size("col")
    share = channels // rows
    half = row_count // 2
    pairs = [(part, part ^ 1) for part in range(parts)]
    first, block, row, inverse, forward, backward = tables(rows * row_count, parts * col_count, row_count, parts)
    near_len = parts * col_count // 2
    mine = rows * row_count // (parts // 2)
    outs = []

    def exchange(array):
        flat = array.reshape((rows * parts,) + array.shape[2:])
        return lax.all_to_all(flat, ("row", "col"), 0, 0, tiled=True).reshape(array.shape)

    for turn in range(share):
        own = slice(turn * rows, (turn + 1) * rows)
        tall = half + 2 * (row_count // parts)
        args = (signal[own], filter_real[own], filter_imag[own], skip[None])
        send, skips, kept = pl.pallas_call(
            pack_kernel,
            out_shape=[
                pltpu.VMEM((rows, parts, tall, col_count), jnp.bfloat16),
                pltpu.VMEM((1, channels), jnp.float32),
                pltpu.VMEM((rows, row_count, col_count), jnp.bfloat16),
            ],
            in_specs=[pl.BlockSpec(memory_space=pltpu.HBM)] * len(args),
            out_specs=[IN_VMEM] * 3,
            scratch_shapes=[pltpu.SemaphoreType.DMA((2 * parts + 2,))],
            compiler_params=PARAMS,
            cost_estimate=pl.CostEstimate(flops=10**9, bytes_accessed=0, transcendentals=0),
        )(*(pltpu.with_memory_space_constraint(arg, pltpu.HBM) for arg in args))
        got = exchange(send)
        swapped = lax.ppermute(got, "col", pairs)
        near = call(
            near_kernel,
            [((2 * mine, 2 * near_len), jnp.float32), ((4, mine, near_len), jnp.float32)],
            *(got, first, block, row, forward),
            flops=10**9,
        )
        (partial_sums,) = call(
            spectrum_kernel,
            [((rows, parts, half, col_count), jnp.bfloat16)],
            *(*near, got, swapped, first, forward, backward, inverse),
        )
        back = exchange(partial_sums)
        outs.append(
            pl.pallas_call(
                functools.partial(finish_kernel, turn=turn),
                out_shape=jax.ShapeDtypeStruct((rows, row_count, col_count), jnp.bfloat16),
                in_specs=[IN_VMEM] * 3,
                compiler_params=PARAMS,
            )(*(pltpu.with_memory_space_constraint(arg, pltpu.VMEM) for arg in (back, kept, skips)))
        )
    return outs[0] if share == 1 else jnp.concatenate(outs, axis=0)


def local(signal, filter_real, filter_imag, skip):
    channels, row_count, col_count = signal.shape
    parts = lax.axis_size("col")
    fits = parts % 2 == 0 and row_count == 8 * parts and col_count % 128 == 0
    if channels % lax.axis_size("row") == 0 and fits:
        return local_by_channels(signal, filter_real, filter_imag, skip)
    return local_by_columns(signal, filter_real, filter_imag, skip)


def solution(mesh):
    in_specs = (P(None, "row", "col"), P(None, "row", "col"), P(None, "row", "col"), P())
    out_specs = P(None, "row", "col")
    return jax.shard_map(local, mesh=mesh, in_specs=in_specs, out_specs=out_specs, check_vma=False)
```

```python
import functools
import math

import jax
import jax.numpy as jnp
import numpy as np
from jax import lax
from jax.experimental import pallas as pl
from jax.experimental.pallas import tpu as pltpu
from jax.sharding import PartitionSpec as P


def phase_table(left_ids, right_ids, modulus):
    product = left_ids[:, None] * right_ids[None, :] % modulus
    angle = -2.0 * math.pi / modulus * product.astype(jnp.float32)
    return (jnp.cos(angle).astype(jnp.bfloat16), jnp.sin(angle).astype(jnp.bfloat16))


def twist_table(left_ids, right_ids, modulus):
    product = left_ids[:, None] * right_ids[None, :] % modulus
    angle = -2.0 * math.pi / modulus * product.astype(jnp.float32)
    return (jnp.cos(angle), jnp.sin(angle))


def column_product(series, phase):
    return jnp.einsum("crn,nk->crk", series, phase, preferred_element_type=jnp.float32)


def row_product(phase, series):
    return jnp.einsum("rn,cnj->crj", phase, series, preferred_element_type=jnp.float32)


def local_by_columns(signal, filter_real, filter_imag, skip):
    channels, row_count, col_count = signal.shape
    first_len = row_count * lax.axis_size("row")
    second_len = col_count * lax.axis_size("col")
    seq_len = first_len * second_len
    row_offset = lax.axis_index("row") * row_count
    col_offset = lax.axis_index("col") * col_count
    own_rows = row_offset + jnp.arange(row_count, dtype=jnp.int32)
    own_cols = col_offset + jnp.arange(col_count, dtype=jnp.int32)
    twist_re, twist_im = twist_table(own_rows, own_cols, seq_len)
    pair_width = col_count // lax.axis_size("row")
    pair_cols = (
        col_offset + lax.axis_index("row") * pair_width + jnp.arange(pair_width, dtype=jnp.int32)
    )
    all_rows = jnp.arange(first_len, dtype=jnp.int32)
    full_re, full_im = phase_table(all_rows, all_rows, first_len)
    columns_whole = lax.all_to_all(signal, "row", split_axis=2, concat_axis=1, tiled=True)
    pair_b_re = row_product(full_re, columns_whole)
    pair_b_im = row_product(full_im, columns_whole)
    pair_tw_re, pair_tw_im = twist_table(all_rows, pair_cols, seq_len)
    pair_mix_re = (pair_b_re * pair_tw_re - pair_b_im * pair_tw_im).astype(jnp.bfloat16)
    pair_mix_im = (pair_b_re * pair_tw_im + pair_b_im * pair_tw_re).astype(jnp.bfloat16)
    mixed_re, mixed_im = (
        lax.all_to_all(pair_mix_re, "row", split_axis=1, concat_axis=2, tiled=True),
        lax.all_to_all(pair_mix_im, "row", split_axis=1, concat_axis=2, tiled=True),
    )
    part_re = lax.all_gather(mixed_re, "col", axis=2, tiled=True)
    part_im = lax.all_gather(mixed_im, "col", axis=2, tiled=True)
    all_cols = jnp.arange(second_len, dtype=jnp.int32)
    phase_re, phase_im = phase_table(all_cols, own_cols, second_len)
    spec_re = column_product(part_re, phase_re) - column_product(part_im, phase_im)
    spec_im = column_product(part_re, phase_im) + column_product(part_im, phase_re)
    prod_re = (spec_re * filter_real - spec_im * filter_imag).astype(jnp.bfloat16)
    prod_im = (spec_re * filter_imag + spec_im * filter_real).astype(jnp.bfloat16)
    part_re = lax.all_gather(prod_re, "col", axis=2, tiled=True)
    part_im = lax.all_gather(prod_im, "col", axis=2, tiled=True)
    new_re = column_product(part_re, phase_re) + column_product(part_im, phase_im)
    new_im = column_product(part_im, phase_re) - column_product(part_re, phase_im)
    unwound_re = (new_re * twist_re + new_im * twist_im).astype(jnp.bfloat16)
    unwound_im = (new_im * twist_re - new_re * twist_im).astype(jnp.bfloat16)
    pair_un_re, pair_un_im = (
        lax.all_to_all(unwound_re, "row", split_axis=2, concat_axis=1, tiled=True),
        lax.all_to_all(unwound_im, "row", split_axis=2, concat_axis=1, tiled=True),
    )
    pair_total = row_product(full_re, pair_un_re) + row_product(full_im, pair_un_im)
    pair_out = (
        pair_total / seq_len + skip[:, None, None] * columns_whole.astype(jnp.float32)
    ).astype(jnp.bfloat16)
    return lax.all_to_all(pair_out, "row", split_axis=1, concat_axis=2, tiled=True)


def row_group(side, member, parts):
    return side + member * (parts - 1 - 2 * side)


def numpy_phase(left_ids, right_ids, modulus):
    product = (left_ids[:, None].astype(np.int64) * right_ids[None, :]) % modulus
    angle = np.float32(-2.0 * math.pi / modulus) * product.astype(np.float32)
    return np.cos(angle), np.sin(angle)


def tables(first_len, second_len, row_count, parts):
    height = row_count // parts
    rows = np.arange(first_len)
    cols = np.arange(second_len)
    by_core = cols.reshape(parts, 2, -1).swapaxes(0, 1).reshape(-1)
    blocks = rows.reshape(-1, row_count)
    groups = [row_group(part // 2, part % 2, parts) for part in range(parts)]
    own = [blocks[:, group * height : (group + 1) * height].reshape(-1) for group in groups]
    first = np.stack(numpy_phase(rows, rows, first_len))
    sides = [[[kind[own[2 * side + core]] for core in range(2)] for kind in first] for side in range(parts // 2)]
    inverse = [
        np.concatenate([kind[:, own[member]] for kind in first for member in (part, part ^ 1)], axis=1)
        for part in range(parts)
    ]
    block_twist = numpy_phase(blocks[:, 0], by_core, first_len * second_len)
    row_twist = numpy_phase(blocks[0], by_core, first_len * second_len)
    forward = np.concatenate(numpy_phase(by_core, cols, second_len), axis=1)
    backward = np.concatenate(numpy_phase(cols, by_core, second_len), axis=1)
    return (
        jnp.asarray(np.array(sides), jnp.bfloat16),
        jnp.asarray(np.stack(block_twist), jnp.float32),
        jnp.asarray(np.stack(row_twist), jnp.float32),
        jnp.asarray(np.stack(inverse), jnp.bfloat16),
        jnp.asarray(forward, jnp.bfloat16),
        jnp.asarray(backward, jnp.bfloat16),
    )


def dot(left, right):
    return jnp.dot(left, right, preferred_element_type=jnp.float32)


def crossed(one, two):
    half = one.shape[-1] // 2
    return (
        jnp.concatenate([one[..., :half], two[..., :half]], axis=-1),
        jnp.concatenate([one[..., half:], two[..., half:]], axis=-1),
    )


def in_left(array):
    axis = array.ndim - 1
    return lax.broadcasted_iota(jnp.int32, array.shape, axis) < array.shape[axis] // 2


def turned_over(array):
    half = array.shape[-1] // 2
    return jnp.concatenate([array[..., half:], array[..., :half]], axis=-1)


def side_and_core():
    part = lax.axis_index("col")
    return part // 2, part % 2


def half_of(core, width):
    return pl.ds(pl.multiple_of(core * width, width), width)


def series_of(ref):
    rows, parts, tall, width = ref.shape
    half = tall // 2
    strips = []
    for part in range(0, parts, 2):
        even, odd = ref[:, part, :half, :], ref[:, part + 1, :half, :]
        left = in_left(even)
        pair = [jnp.where(left, even, odd), turned_over(jnp.where(left, odd, even))]
        strips.append(jnp.concatenate(pair, axis=1).reshape(rows * 2 * half, width))
    return jnp.concatenate(strips, axis=1)


def filter_of(ref, start, count):
    rows, parts, _, width = ref.shape
    return jnp.concatenate(
        [ref[:, part, start : start + count, :].astype(jnp.float32).reshape(rows * count, width) for part in range(parts)],
        axis=1,
    )


def twists(block_ref, row_ref, height, side, core, span):
    block_re, block_im = block_ref[0, :, span][:, None, :], block_ref[1, :, span][:, None, :]
    shape = (block_ref.shape[1] * height, span.size)
    re, im = [], []
    for member in (core, 1 - core):
        group = row_group(side, member, row_ref.shape[1] // height)
        at = pl.ds(pl.multiple_of(group * height, height), height)
        row_re, row_im = row_ref[0, at, span][None], row_ref[1, at, span][None]
        re.append((block_re * row_re - block_im * row_im).reshape(shape))
        im.append((block_re * row_im + block_im * row_re).reshape(shape))
    return jnp.concatenate(re, axis=0), jnp.concatenate(im, axis=0)


def turned(re, im, by_re, by_im):
    return re * by_re - im * by_im, re * by_im + im * by_re


def widened(pair):
    re, im = (each.astype(jnp.bfloat16) for each in pair)
    return jnp.concatenate([jnp.concatenate([re, -im], axis=1), jnp.concatenate([im, re], axis=1)], axis=0)


def widened_back(pair):
    re, im = (each.astype(jnp.bfloat16) for each in pair)
    return jnp.concatenate([jnp.concatenate([re, im], axis=1), jnp.concatenate([im, -re], axis=1)], axis=0)


def pack_kernel(signal_ref, real_ref, imag_ref, skip_ref, send_ref, skips_ref, kept_ref, real_buf, imag_buf, sems):
    _, parts, _, _ = send_ref.shape
    row_count = signal_ref.shape[-2]
    half = row_count // 2
    height = row_count // parts
    moves = ((signal_ref, kept_ref), (real_ref, real_buf), (imag_ref, imag_buf), (skip_ref, skips_ref))
    copies = [pltpu.make_async_copy(a, b, sems.at[i]) for i, (a, b) in enumerate(moves)]
    for copy in copies:
        copy.start()
    copies[0].wait()
    is_even = side_and_core()[1] == 0
    upper, lower = kept_ref[:, :half], kept_ref[:, half:]
    halves = crossed(jnp.where(is_even, upper, lower), jnp.where(is_even, lower, upper))
    for part in range(parts):
        send_ref[:, part, :half] = halves[part % 2]
    for buf, copy, start in ((real_buf, copies[1], half), (imag_buf, copies[2], half + height)):
        copy.wait()
        for part in range(parts):
            group = row_group(part // 2, part % 2, parts)
            send_ref[:, part, start : start + height] = buf[:, group * height : (group + 1) * height]
    copies[3].wait()


def half_transform(ref, first_ref, side, core):
    left = [first_ref[side, kind, member] for kind in range(2) for member in (core, 1 - core)]
    both = dot(jnp.concatenate(left, axis=0), series_of(ref))
    mine = both.shape[0] // 2
    return both[:mine], both[mine:]


def forward_rows(forward_ref, core):
    second_len = forward_ref.shape[0]
    rows = half_of(core, second_len // 2)
    return jnp.concatenate([forward_ref[rows, :second_len], forward_ref[rows, second_len:]], axis=0)


def near_kernel(got_ref, first_ref, block_ref, row_ref, forward_ref, spec_ref, twist_ref):
    tall = got_ref.shape[2]
    side, core = side_and_core()
    first_len, second_len = first_ref.shape[-1], forward_ref.shape[0]
    height = tall // 4
    near_len = second_len // 2
    twist = twists(block_ref, row_ref, height, side, core, half_of(core, near_len))
    mixed = turned(*half_transform(got_ref, first_ref, side, core), *twist)
    spec_ref[...] = dot(widened(mixed), forward_rows(forward_ref, core))
    twist_ref[0], twist_ref[1] = twists(block_ref, row_ref, height, side, core, half_of(1 - core, near_len))
    twist_ref[2], twist_ref[3] = (each / (first_len * second_len) for each in twist)


def spectrum_kernel(spec_ref, twist_ref, got_ref, swapped_ref, first_ref, forward_ref, backward_ref, inverse_ref, out_ref):
    rows, parts, tall, width = got_ref.shape
    side, core = side_and_core()
    half, height = tall // 2, tall // 4
    second_len = forward_ref.shape[0]
    near_len = second_len // 2
    mixed = turned(*half_transform(swapped_ref, first_ref, side, core), twist_ref[0], twist_ref[1])
    spec = spec_ref[...] + dot(widened(mixed), forward_rows(forward_ref, 1 - core))
    mine = spec.shape[0] // 2
    filt_re, filt_im = (
        jnp.concatenate([filter_of(ref, start, height) for ref in (got_ref, swapped_ref)], axis=0)
        for start in (half, half + height)
    )
    prod = turned(spec[:mine], spec[mine:], filt_re, filt_im)
    cols = [pl.ds(pl.multiple_of(at + core * near_len, near_len), near_len) for at in (0, second_len)]
    back = dot(widened_back(prod), jnp.concatenate([backward_ref[:, col] for col in cols], axis=0))
    unwound = turned(back[:mine], back[mine:], twist_ref[2], -twist_ref[3])
    unwound = jnp.concatenate(unwound, axis=0).astype(jnp.bfloat16)
    total = dot(inverse_ref[lax.axis_index("col")], unwound).astype(jnp.bfloat16)
    for place in range(parts // 2):
        piece = total[:, place * width : (place + 1) * width].reshape(rows, 2 * half, width)
        upper, lower = piece[:, :half], turned_over(piece[:, half:])
        left = in_left(upper)
        out_ref[:, 2 * place] = jnp.where(left, upper, lower)
        out_ref[:, 2 * place + 1] = jnp.where(left, lower, upper)


def finish_kernel(back_ref, kept_ref, skips_ref, out_ref, *, turn):
    rows, parts, half, _ = back_ref.shape
    cores = []
    for core in range(2):
        shares = [back_ref[:, part].astype(jnp.float32) for part in range(core, parts, 2)]
        cores.append(sum(shares[1:], shares[0]))
    one, two = crossed(*cores)
    is_even = side_and_core()[1] == 0
    sums = jnp.concatenate([jnp.where(is_even, one, two), jnp.where(is_even, two, one)], axis=1)
    for channel in range(rows):
        at = turn * rows + channel
        term = skips_ref[:, at : at + 1] * kept_ref[channel].astype(jnp.float32)
        out_ref[channel] = (sums[channel] + term).astype(jnp.bfloat16)


PARAMS = pltpu.CompilerParams(vmem_limit_bytes=8 * 2**20)
IN_VMEM = pl.BlockSpec(memory_space=pltpu.VMEM)


def call(kernel, outs, *args, flops=None):
    return pl.pallas_call(
        kernel,
        out_shape=[pltpu.VMEM(shape, kind) for shape, kind in outs],
        in_specs=[IN_VMEM] * len(args),
        out_specs=[IN_VMEM] * len(outs),
        compiler_params=PARAMS,
        cost_estimate=flops and pl.CostEstimate(flops=flops, bytes_accessed=0, transcendentals=0),
    )(*(pltpu.with_memory_space_constraint(arg, pltpu.VMEM) for arg in args))


def local_by_channels(signal, filter_real, filter_imag, skip):
    channels, row_count, col_count = signal.shape
    rows = lax.axis_size("row")
    parts = lax.axis_size("col")
    share = channels // rows
    half = row_count // 2
    pairs = [(part, part ^ 1) for part in range(parts)]
    first, block, row, inverse, forward, backward = tables(rows * row_count, parts * col_count, row_count, parts)
    near_len = parts * col_count // 2
    mine = rows * row_count // (parts // 2)
    outs = []

    def exchange(array):
        flat = array.reshape((rows * parts,) + array.shape[2:])
        return lax.all_to_all(flat, ("row", "col"), 0, 0, tiled=True).reshape(array.shape)

    for turn in range(share):
        own = slice(turn * rows, (turn + 1) * rows)
        tall = half + 2 * (row_count // parts)
        args = (signal[own], filter_real[own], filter_imag[own], skip[None])
        send, skips, kept = pl.pallas_call(
            pack_kernel,
            out_shape=[
                pltpu.VMEM((rows, parts, tall, col_count), jnp.bfloat16),
                pltpu.VMEM((1, channels), jnp.float32),
                pltpu.VMEM((rows, row_count, col_count), jnp.bfloat16),
            ],
            in_specs=[pl.BlockSpec(memory_space=pltpu.HBM)] * len(args),
            out_specs=[IN_VMEM] * 3,
            scratch_shapes=[
                *[pltpu.VMEM((rows, row_count, col_count), jnp.bfloat16)] * 2,
                pltpu.SemaphoreType.DMA((4,)),
            ],
            compiler_params=PARAMS,
            cost_estimate=pl.CostEstimate(flops=10**9, bytes_accessed=0, transcendentals=0),
        )(*(pltpu.with_memory_space_constraint(arg, pltpu.HBM) for arg in args))
        got = exchange(send)
        swapped = lax.ppermute(got, "col", pairs)
        near = call(
            near_kernel,
            [((2 * mine, 2 * near_len), jnp.float32), ((4, mine, near_len), jnp.float32)],
            *(got, first, block, row, forward),
            flops=10**9,
        )
        (partial_sums,) = call(
            spectrum_kernel,
            [((rows, parts, half, col_count), jnp.bfloat16)],
            *(*near, got, swapped, first, forward, backward, inverse),
        )
        back = exchange(partial_sums)
        outs.append(
            pl.pallas_call(
                functools.partial(finish_kernel, turn=turn),
                out_shape=jax.ShapeDtypeStruct((rows, row_count, col_count), jnp.bfloat16),
                in_specs=[IN_VMEM] * 3,
                compiler_params=PARAMS,
            )(*(pltpu.with_memory_space_constraint(arg, pltpu.VMEM) for arg in (back, kept, skips)))
        )
    return outs[0] if share == 1 else jnp.concatenate(outs, axis=0)


def local(signal, filter_real, filter_imag, skip):
    channels, row_count, col_count = signal.shape
    parts = lax.axis_size("col")
    fits = parts % 2 == 0 and row_count == 8 * parts and col_count % 128 == 0
    if channels % lax.axis_size("row") == 0 and fits:
        return local_by_channels(signal, filter_real, filter_imag, skip)
    return local_by_columns(signal, filter_real, filter_imag, skip)


def solution(mesh):
    in_specs = (P(None, "row", "col"), P(None, "row", "col"), P(None, "row", "col"), P())
    out_specs = P(None, "row", "col")
    return jax.shard_map(local, mesh=mesh, in_specs=in_specs, out_specs=out_specs, check_vma=False)
```
